256 devices in a mesh: rows: 64 (over x, z, core), cols: 4 (over y).
Axes of the slice: x: 4, y: 4, z: 8, core: 2. Of those that a mesh axis runs over, the one named last changes fastest.
Arguments:
- column_lists: int32 [256, 13], replicated, may hold values from -1 to 255, as said below
- block_values: bfloat16 [256, 13, 128, 128], P('rows'), as said below
Outputs:
- purified: bfloat16 [256, 13, 128, 128], P('rows', None, None, 'cols')
The draws below stay inside these ranges and needn't reach their ends.
Inputs may be any that keep to these rules, and one draw needn't show every extreme that they name: `column_lists`: slot (13 - 1) // 2 of row i holds i. Slot s of row i holds -1 or a row j, and then slot 12 - s of row j holds i. There is an ordering of the rows, taken cyclically, in which the row in slot s of row i stands s - (13 - 1) // 2 places after row i. With owners the aligned groups of 4 rows, the slots of one owner's rows hold at most 2 rows of any one other owner, and some pair of owners has exactly 2. Over the slots s of one owner's rows that hold rows of one other owner, the sum of 13 - |s - (13 - 1) // 2| is at most 16, and exactly 16 for some pair of owners. block_values[j, 12 - s] is the transpose of block_values[i, s] where slot s of row i holds j; blocks of empty slots are zero.
All inputs are finite; a program needn't handle non-finite values.
Results may differ from the reference program's by a relative error of at most 0.0039.
Values may be sent and summed in bfloat16 or wider, within the bound.
No kernel may reach another device: no remote copies, remote signals or barrier semaphores. Data moves between devices by JAX's collectives and lax.ppermute only.
A program may use at most 128 MiB of HBM per device.

```python
import jax
import jax.numpy as jnp
from jax import lax

BLK = 128
SLOTS = 13
CAP = 2
BAND = 16
RB_DEV = 4
NB = 256
N_ROWS = 64


def pattern_tables(key):
    all_rows = RB_DEV * N_ROWS
    middle = (SLOTS - 1) // 2
    key_owner, key_order, key_keep = jax.random.split(key, 3)
    owners = jax.random.permutation(key_owner, N_ROWS).astype(jnp.int32)
    first_owner = owners[0]
    second_owner = owners[1]
    chosen = jnp.stack([first_owner * RB_DEV, second_owner * RB_DEV, second_owner * RB_DEV + 1]).astype(jnp.int32)
    scores = jax.random.permutation(key_order, all_rows).astype(jnp.int32)
    scores = scores.at[chosen].set(jnp.arange(3, dtype=jnp.int32) - 3)
    first_order = jnp.argsort(scores, stable=True).astype(jnp.int32)
    ordering = jnp.concatenate([first_order[0:1], first_order[3:6], first_order[1:2], first_order[6:7], first_order[2:3], first_order[7:]])
    place = jnp.arange(all_rows, dtype=jnp.int32)[:, None]
    offset = jnp.arange(1, middle + 1, dtype=jnp.int32)[None, :]
    left_row = jnp.broadcast_to(ordering[:, None], (all_rows, middle))
    right_row = ordering[(place + offset) % all_rows]
    rate_left = (4 * all_rows - 2 * left_row) * 64 // (4 * all_rows)
    rate_right = (4 * all_rows - 2 * right_row) * 64 // (4 * all_rows)
    keep_level = rate_left * rate_right // 64
    ticket = jax.random.randint(key_keep, (all_rows, middle), 0, 64).astype(jnp.int32)
    forced = (place == 0) & ((offset == 4) | (offset == 6))
    wanted = forced | (ticket < keep_level) & (place != 0)
    owner_left = left_row // RB_DEV
    owner_right = right_row // RB_DEV
    crossing = owner_left != owner_right
    pair_key = jnp.minimum(owner_left, owner_right) * N_ROWS + jnp.maximum(owner_left, owner_right)
    keyed = jnp.where(wanted & crossing, pair_key, N_ROWS * N_ROWS).reshape(-1).astype(jnp.int32)
    edge_count = all_rows * middle
    sort_order = jnp.argsort(keyed, stable=True).astype(jnp.int32)
    sorted_key = keyed[sort_order]
    positions = jnp.arange(edge_count, dtype=jnp.int32)
    changed = jnp.concatenate([jnp.ones((1,), dtype=bool), sorted_key[1:] != sorted_key[:-1]])
    group_starts = jnp.where(changed, positions, 0)
    group_first = lax.cummax(group_starts, axis=0)
    edge_rank = jnp.zeros((edge_count,), jnp.int32).at[sort_order].set(positions - group_first).reshape(all_rows, middle)
    edge_weight = jnp.broadcast_to(SLOTS - offset, (all_rows, middle)).reshape(-1).astype(jnp.int32)
    sorted_weight = edge_weight[sort_order]
    running_weight = jnp.cumsum(sorted_weight).astype(jnp.int32)
    group_base = running_weight[group_first] - sorted_weight[group_first]
    edge_load = jnp.zeros((edge_count,), jnp.int32).at[sort_order].set(running_weight - group_base).reshape(all_rows, middle)
    kept_edge = wanted & (~crossing | (edge_rank < CAP) & (edge_load <= BAND))
    edge_id = place * middle + offset - 1
    row_ids = jnp.arange(all_rows, dtype=jnp.int32)
    column_table = jnp.full((all_rows, SLOTS), -1, jnp.int32).at[:, middle].set(row_ids)
    column_table = column_table.at[left_row, middle + offset].set(jnp.where(kept_edge, right_row, -1))
    column_table = column_table.at[right_row, middle - offset].set(jnp.where(kept_edge, left_row, -1))
    identity = jnp.full((all_rows, SLOTS), 0, jnp.int32).at[:, middle].set(edge_count + row_ids)
    identity = identity.at[left_row, middle + offset].set(edge_id)
    identity = identity.at[right_row, middle - offset].set(edge_id)
    transposed = jnp.zeros((all_rows, SLOTS), dtype=bool).at[right_row, middle - offset].set(True)
    return (column_table, identity, transposed)


def draw_column_lists(key, part):
    return pattern_tables(jax.random.fold_in(key, 7))[0]


def draw_block_values(key, part):
    column_table, identity, transposed = pattern_tables(jax.random.fold_in(key, 7))
    all_rows = RB_DEV * N_ROWS
    middle = (SLOTS - 1) // 2
    key_vals = jax.random.fold_in(key, 8)
    spread = 0.15

    def one_block(block_id):
        block_key = jax.random.fold_in(key_vals, block_id)
        sampled = jax.random.normal(block_key, (BLK, BLK))
        return sampled

    def one_row(row_index):
        block_ids = identity[row_index]
        flips = transposed[row_index]
        sampled = jax.vmap(one_block)(block_ids)
        sampled = jnp.where(flips[:, None, None], jnp.swapaxes(sampled, 1, 2), sampled)
        symmetric = (sampled + jnp.swapaxes(sampled, 1, 2)) * 0.70710678
        centre = (jnp.arange(SLOTS) == middle)[:, None, None]
        sampled = jnp.where(centre, symmetric, sampled)
        factor = spread * jnp.ones((SLOTS,), jnp.float32)
        sampled = sampled * factor[:, None, None]
        return jnp.where((column_table[row_index] >= 0)[:, None, None], sampled, 0.0)
    return lax.map(one_row, jnp.arange(all_rows, dtype=jnp.int32)).astype(jnp.bfloat16)


def setup_inputs(seed: int = 0) -> dict:
    seeds = jax.random.split(jax.random.key(seed), 3)
    return {
        "column_lists": draw_column_lists(jax.random.fold_in(seeds[2], 71), 0),
        "block_values": draw_block_values(jax.random.fold_in(seeds[2], 71), 0),
    }


def reference(column_lists, block_values):
    present = column_lists >= 0
    target = jnp.maximum(column_lists, 0)
    masked = jnp.where(present[:, :, None, None], block_values, jnp.zeros((), jnp.bfloat16))

    def one_row(row_index):
        own_cols = column_lists[row_index]
        own_present = present[row_index]
        partners = target[row_index]
        partner_blocks = masked[partners].astype(jnp.float32)
        partner_cols = column_lists[partners]
        partner_present = present[partners]
        matches = (partner_cols[:, None, :] == own_cols[None, :, None]) & partner_present[:, None, :]
        matches = matches & own_present[:, None, None] & own_present[None, :, None]
        windows = jnp.einsum("asb,abpq->aspq", matches.astype(jnp.float32), partner_blocks, precision=lax.Precision.HIGHEST)
        own_blocks = masked[row_index].astype(jnp.float32)
        square_sum = jnp.einsum("apq,asqr->spr", own_blocks, windows, precision=lax.Precision.HIGHEST)
        square = jnp.where(own_present[:, None, None], square_sum, 0.0).astype(jnp.bfloat16)
        cube_sum = jnp.einsum("apq,asqr->spr", square.astype(jnp.float32), windows, precision=lax.Precision.HIGHEST)
        purified = jnp.where(own_present[:, None, None], 3.0 * square.astype(jnp.float32) - 2.0 * cube_sum, 0.0)
        return purified.astype(jnp.bfloat16)

    return lax.map(one_row, jnp.arange(NB, dtype=jnp.int32))
```

```python
import functools

import jax
import jax.numpy as jnp
import numpy as np
from jax import lax
from jax.experimental import pallas as pl
from jax.experimental.pallas import tpu as pltpu
from jax.sharding import Mesh
from jax.sharding import PartitionSpec as P

X, Z, CORE, Y = 4, 8, 2, 4
BLK = 128
SLOTS = 13
MID = 6
HALF = 7
ROWS_HERE = 4
PIECES = X * Y
TILE = BLK // PIECES
AXES = ("x", "z", "core", "y")


def wanted():
    pairs = []
    for a in range(SLOTS):
        if a == MID:
            continue
        for s in range(a, min(SLOTS, a + HALF)):
            if s != MID:
                pairs.append((a, s))
    return pairs


WANTED = wanted()
COUNT = len(WANTED)


def runs():
    out = []
    for place, (a, s) in enumerate(WANTED):
        d = s - a
        if out and out[-1][0] == a and out[-1][1] + out[-1][2] == d:
            out[-1][2] += 1
        else:
            out.append([a, d, 1, place])
    return [tuple(r) for r in out]


RUNS = runs()


def select_kernel(lists, where, *refs):
    pieces = refs[: 2 * Z]
    out, held, sems = refs[2 * Z :]
    z, core = where[1], where[2]
    copies = []
    for n in range(2 * Z):
        step, other = n % Z, n // Z
        place = lax.rem(z + step, Z) + Z * lax.rem(core + other, 2)
        copies.append(pltpu.make_async_copy(pieces[n], held.at[place], sems.at[n]))
    for copy in copies:
        copy.start()
    for copy in copies:
        copy.wait()

    def one(t, carry):
        owner = ((t // Y) * Z + z) * CORE + core
        row = ROWS_HERE * owner + lax.rem(t, Y)
        for a, d, length, first in RUNS:
            k = jnp.maximum(lists[row * SLOTS + a], 0)
            r = k // ROWS_HERE
            place = lax.rem(r, 2) * Z + lax.rem(r // 2, Z)
            inner = (r // (2 * Z)) * ROWS_HERE + lax.rem(k, ROWS_HERE)
            out[t, first : first + length] = held[place, inner, d : d + length]
        return carry

    lax.fori_loop(0, PIECES, one, 0)


def select(lists, where, pieces):
    smem = pl.BlockSpec(memory_space=pltpu.SMEM)
    hbm = pl.BlockSpec(memory_space=pl.ANY)
    return pl.pallas_call(
        select_kernel,
        out_shape=jax.ShapeDtypeStruct((PIECES, COUNT, TILE, BLK), jnp.bfloat16),
        in_specs=[smem, smem] + [hbm] * (2 * Z),
        out_specs=pl.BlockSpec(memory_space=pltpu.VMEM),
        scratch_shapes=[
            pltpu.VMEM((2 * Z, X * ROWS_HERE, HALF, TILE, BLK), jnp.bfloat16),
            pltpu.SemaphoreType.DMA((2 * Z,)),
        ],
        name="select",
    )(lists, where, *pieces)


def groups():
    out = []
    for s in range(0, SLOTS, 2):
        n = min(2, SLOTS - s)
        low = max(0, s - MID)
        high = min(SLOTS - 1, s + n - 1 + MID)
        out.append((s, n, low, high - low + 1))
    return out


GROUPS = groups()


def purify_kernel(lists, where, got, own, out, u, w, sq, sems):
    row = ROWS_HERE * ((where[0] * Z + where[1]) * CORE + where[2]) + where[3]
    copies = [pltpu.make_async_copy(got.at[p], u.at[:, p], sems.at[p]) for p in range(PIECES)]
    for s in range(SLOTS):
        copies.append(
            pltpu.make_async_copy(
                own.at[where[3], s],
                w.at[MID * BLK : (MID + 1) * BLK, s * BLK : (s + 1) * BLK],
                sems.at[PIECES + s],
            )
        )
    for copy in copies:
        copy.start()

    def blk(a):
        return slice(a * BLK, (a + 1) * BLK)

    for a in range(SLOTS - HALF):
        w[blk(a), blk(a + HALF)] = jnp.zeros((BLK, BLK), jnp.bfloat16)
        w[blk(a + HALF), blk(a)] = jnp.zeros((BLK, BLK), jnp.bfloat16)
    for copy in copies:
        copy.wait()
    for s in range(SLOTS):
        if s != MID:
            w[blk(s), blk(MID)] = w[blk(MID), blk(s)].T
    for place, (a, s) in enumerate(WANTED):
        value = u[place].reshape(BLK, BLK)
        w[blk(a), blk(s)] = value
        if a != s:
            w[blk(s), blk(a)] = value.T

    def mask(value, s):
        return jnp.where(lists[row * SLOTS + s] >= 0, value, jnp.zeros_like(value))

    def span(first, n):
        return slice(first * BLK, (first + n) * BLK)

    for s, n, low, count in GROUPS:
        total = jnp.dot(
            w[blk(MID), span(low, count)], w[span(low, count), span(s, n)], preferred_element_type=jnp.float32
        )
        for j in range(n):
            sq[:, blk(s + j)] = mask(total[:, blk(j)], s + j).astype(jnp.bfloat16)
    for s, n, low, count in GROUPS:
        total = jnp.dot(sq[:, span(low, count)], w[span(low, count), span(s, n)], preferred_element_type=jnp.float32)
        for j in range(n):
            value = 3.0 * sq[:, blk(s + j)].astype(jnp.float32) - 2.0 * total[:, blk(j)]
            value = mask(value, s + j).T.astype(jnp.bfloat16)
            for part in range(Y):
                out[part, s + j] = value[part * 32 : (part + 1) * 32]


def purify(lists, where, got, own):
    smem = pl.BlockSpec(memory_space=pltpu.SMEM)
    hbm = pl.BlockSpec(memory_space=pl.ANY)
    return pl.pallas_call(
        purify_kernel,
        out_shape=jax.ShapeDtypeStruct((Y, SLOTS, BLK // Y, BLK), jnp.bfloat16),
        in_specs=[smem, smem, hbm, hbm],
        out_specs=pl.BlockSpec(memory_space=pltpu.VMEM),
        scratch_shapes=[
            pltpu.VMEM((COUNT, PIECES, TILE, BLK), jnp.bfloat16),
            pltpu.VMEM((SLOTS * BLK, SLOTS * BLK), jnp.bfloat16),
            pltpu.VMEM((BLK, SLOTS * BLK), jnp.bfloat16),
            pltpu.SemaphoreType.DMA((PIECES + SLOTS,)),
        ],
        name="purify",
    )(lists, where, got, own)


def shift(value, axis, size, step):
    return lax.ppermute(value, axis, [((i + step) % size, i) for i in range(size)])


def gather_z(own):
    up, down = [own], [own]
    for _ in range(3):
        up.append(shift(up[-1], "z", Z, 1))
        down.append(shift(down[-1], "z", Z, -1))
    half = own.shape[0] // 2
    far = jnp.concatenate([shift(up[3][:half], "z", Z, 1), shift(down[3][half:], "z", Z, -1)], 0)
    return [own, up[1], up[2], up[3], far, down[3], down[2], down[1]]


def body(column_lists, block_values):
    lists = column_lists.reshape(-1)
    where = jnp.stack([lax.axis_index(a) for a in AXES]).astype(jnp.int32)
    tiles = block_values[:, MID:].reshape(ROWS_HERE, HALF, X, Y, TILE, BLK)
    mine = lax.dynamic_index_in_dim(tiles, where[3], 3, keepdims=False)
    mine = mine.transpose(2, 0, 1, 3, 4)
    part = lax.all_to_all(mine, "x", 0, 0, tiled=True)
    part = part.reshape(X * ROWS_HERE, HALF, TILE, BLK)
    here = gather_z(part)
    there = [shift(p, "core", CORE, 1) for p in here]
    asked = select(lists, where, here + there)
    got = lax.all_to_all(asked, ("x", "y"), 0, 0, tiled=True)
    strips = purify(lists, where, got, block_values)
    mixed = lax.all_to_all(strips, "y", 0, 0, tiled=True)
    return mixed.transpose(0, 1, 3, 2)


def solution(mesh):
    fine = Mesh(mesh.devices.reshape(X, Z, CORE, Y), AXES)
    rows = ("x", "z", "core")
    return jax.shard_map(
        body, mesh=fine, in_specs=(P(), P(rows)), out_specs=P(rows, None, None, "y"), check_vma=False
    )
```

```python
import jax
import jax.numpy as jnp
from jax import lax
from jax.experimental import pallas as pl
from jax.experimental.pallas import tpu as pltpu
from jax.sharding import Mesh
from jax.sharding import PartitionSpec as P

X, ZL, ZP, CORE, Y = 4, 4, 2, 2, 4
Z = ZL * ZP
BLK = 128
SLOTS = 13
MID = 6
HALF = 7
ROWS_HERE = 4
TILES = X * Y
TILE = BLK // TILES
DESTS = X * ZP * Y
OWNERS = X * Z
CLASSES = ((0, 2, 4, 6), (1, 3, 5, 6))
USED = ((0, 2, 4), (1, 3, 5, 6))
DEPTH = 4
AXES = ("x", "zl", "zp", "core", "y")


def wanted(cls):
    return [
        (a, a + d) for a in range(SLOTS) for d in USED[cls] if a != MID and a + d != MID and a + d < SLOTS
    ]


WANTED = (wanted(0), wanted(1))
COUNT = max(len(w) for w in WANTED)


def runs(cls):
    out = {}
    for place, (a, s) in enumerate(WANTED[cls]):
        j = CLASSES[cls].index(s - a)
        mine = out.setdefault(a, [])
        if mine and mine[-1][0] + mine[-1][1] == j:
            mine[-1][1] += 1
        else:
            mine.append([j, 1, place])
    return list(out.items())


SMEM = pl.BlockSpec(memory_space=pltpu.SMEM)
ANY = pl.BlockSpec(memory_space=pl.ANY)


def pack_kernel(values, out, stage, sems, out_sems):
    y = lax.axis_index("y")
    copies = []
    for x in range(X):
        for zp in range(ZP):
            for j, d in enumerate(CLASSES[zp]):
                rows = pl.ds(pl.multiple_of((x * Y + y) * TILE, TILE), TILE)
                n = len(copies)
                copies.append(
                    pltpu.make_async_copy(values.at[:, MID + d, rows], stage.at[x, zp, :, j], sems.at[n])
                )
    for copy in copies:
        copy.start()
    for copy in copies:
        copy.wait()
    copies = [pltpu.make_async_copy(stage, out.at[:, zl], out_sems.at[zl]) for zl in range(ZL)]
    for copy in copies:
        copy.start()
    for copy in copies:
        copy.wait()


def pack(values):
    shape = (X, ZP, ROWS_HERE, DEPTH, TILE, BLK)
    return pl.pallas_call(
        pack_kernel,
        out_shape=jax.ShapeDtypeStruct((X, ZL) + shape[1:], jnp.bfloat16),
        in_specs=[ANY],
        out_specs=ANY,
        scratch_shapes=[
            pltpu.VMEM(shape, jnp.bfloat16),
            pltpu.SemaphoreType.DMA((X * ZP * DEPTH,)),
            pltpu.SemaphoreType.DMA((ZL,)),
        ],
        name="pack",
    )(values)


def select_kernel(lists, here, there, out, held, sems):
    zl, zp, core = (lax.axis_index(a) for a in ("zl", "zp", "core"))
    copies = [
        pltpu.make_async_copy(here, held.at[core], sems.at[0]),
        pltpu.make_async_copy(there, held.at[1 - core], sems.at[1]),
    ]
    for copy in copies:
        copy.start()
    for copy in copies:
        copy.wait()

    def run(cls):
        def one(t, carry):
            owner = ((t // (ZP * Y)) * Z + 2 * zl + lax.rem(t // Y, ZP)) * CORE + core
            row = ROWS_HERE * owner + lax.rem(t, Y)
            for a, parts in runs(cls):
                k = jnp.maximum(lists[a, row], 0)
                k_core = lax.rem(k // ROWS_HERE, CORE)
                k_owner = k // (ROWS_HERE * CORE)
                k_row = lax.rem(k, ROWS_HERE)
                for j, length, place in parts:
                    out[t, place : place + length] = held[k_core, k_owner, k_row, j : j + length]
            return carry

        lax.fori_loop(0, DESTS, one, 0)

    pl.when(zp == 0)(lambda: run(0))
    pl.when(zp == 1)(lambda: run(1))


def select(lists, here, there):
    return pl.pallas_call(
        select_kernel,
        out_shape=jax.ShapeDtypeStruct((DESTS, COUNT, TILE, BLK), jnp.bfloat16),
        in_specs=[SMEM, ANY, ANY],
        out_specs=pl.BlockSpec(memory_space=pltpu.VMEM),
        scratch_shapes=[
            pltpu.VMEM((CORE, OWNERS, ROWS_HERE, DEPTH, TILE, BLK), jnp.bfloat16),
            pltpu.SemaphoreType.DMA((2,)),
        ],
        name="select",
    )(lists, here, there)


def groups():
    out = []
    for s in range(0, SLOTS, 2):
        n = min(2, SLOTS - s)
        low = max(0, s - MID)
        high = min(SLOTS - 1, s + n - 1 + MID)
        out.append((s, n, low, high - low + 1))
    return out


GROUPS = groups()


def purify_kernel(lists, got, own, out, u, w, sq, sems):
    x, zl, zp, core, y = (lax.axis_index(a) for a in AXES)
    row = ROWS_HERE * ((x * Z + 2 * zl + zp) * CORE + core) + y
    copies = []
    for p in range(DESTS):
        tile = (p // (ZP * Y)) * Y + p % Y
        copies.append(pltpu.make_async_copy(got.at[p], u.at[(p // Y) % ZP, :, tile], sems.at[p]))
    for s in range(SLOTS):
        copies.append(
            pltpu.make_async_copy(
                own.at[y, s],
                w.at[MID * BLK : (MID + 1) * BLK, s * BLK : (s + 1) * BLK],
                sems.at[DESTS + s],
            )
        )
    for copy in copies:
        copy.start()

    def blk(a):
        return slice(a * BLK, (a + 1) * BLK)

    for a in range(SLOTS - HALF):
        w[blk(a), blk(a + HALF)] = jnp.zeros((BLK, BLK), jnp.bfloat16)
        w[blk(a + HALF), blk(a)] = jnp.zeros((BLK, BLK), jnp.bfloat16)
    for copy in copies:
        copy.wait()
    for s in range(SLOTS):
        if s != MID:
            w[blk(s), blk(MID)] = w[blk(MID), blk(s)].T
    for cls in range(ZP):
        for place, (a, s) in enumerate(WANTED[cls]):
            value = u[cls, place].reshape(BLK, BLK)
            w[blk(a), blk(s)] = value
            if a != s:
                w[blk(s), blk(a)] = value.T

    def mask(value, s):
        return jnp.where(lists[s, row] >= 0, value, jnp.zeros_like(value))

    def span(first, n):
        return slice(first * BLK, (first + n) * BLK)

    for s, n, low, count in GROUPS:
        total = jnp.dot(
            w[blk(MID), span(low, count)], w[span(low, count), span(s, n)], preferred_element_type=jnp.float32
        )
        for j in range(n):
            sq[:, blk(s + j)] = mask(total[:, blk(j)], s + j).astype(jnp.bfloat16)
    for s, n, low, count in GROUPS:
        total = jnp.dot(sq[:, span(low, count)], w[span(low, count), span(s, n)], preferred_element_type=jnp.float32)
        for j in range(n):
            value = 3.0 * sq[:, blk(s + j)].astype(jnp.float32) - 2.0 * total[:, blk(j)]
            value = mask(value, s + j).T.astype(jnp.bfloat16)
            for part in range(Y):
                out[part, s + j] = value[part * (BLK // Y) : (part + 1) * (BLK // Y)]


def purify(lists, got, own):
    return pl.pallas_call(
        purify_kernel,
        out_shape=jax.ShapeDtypeStruct((Y, SLOTS, BLK // Y, BLK), jnp.bfloat16),
        in_specs=[SMEM, ANY, ANY],
        out_specs=pl.BlockSpec(memory_space=pltpu.VMEM),
        scratch_shapes=[
            pltpu.VMEM((ZP, COUNT, TILES, TILE, BLK), jnp.bfloat16),
            pltpu.VMEM((SLOTS * BLK, SLOTS * BLK), jnp.bfloat16),
            pltpu.VMEM((BLK, SLOTS * BLK), jnp.bfloat16),
            pltpu.SemaphoreType.DMA((DESTS + SLOTS,)),
        ],
        name="purify",
    )(lists, got, own)


def body(column_lists, block_values):
    lists = column_lists.T
    mine = pack(block_values).reshape(OWNERS, ROWS_HERE, DEPTH, TILE, BLK)
    here = lax.all_to_all(mine, ("x", "zl", "zp"), 0, 0, tiled=True)
    there = lax.ppermute(here, "core", [(0, 1), (1, 0)])
    asked = select(lists, here, there)
    got = lax.all_to_all(asked, ("x", "zp", "y"), 0, 0, tiled=True)
    strips = purify(lists, got, block_values)
    mixed = lax.all_to_all(strips, "y", 0, 0, tiled=True)
    return mixed.transpose(0, 1, 3, 2)


def solution(mesh):
    fine = Mesh(mesh.devices.reshape(X, ZL, ZP, CORE, Y), AXES)
    rows = ("x", "zl", "zp", "core")
    return jax.shard_map(
        body, mesh=fine, in_specs=(P(), P(rows)), out_specs=P(rows, None, None, "y"), check_vma=False
    )
```

```python
import jax
import jax.numpy as jnp
from jax import lax
from jax.experimental import pallas as pl
from jax.experimental.pallas import tpu as pltpu
from jax.sharding import Mesh
from jax.sharding import PartitionSpec as P

X, ZL, ZP, CORE, Y = 4, 4, 2, 2, 4
Z = ZL * ZP
BLK = 128
SLOTS = 13
MID = 6
HALF = 7
ROWS_HERE = 4
TILES = X * Y
TILE = BLK // TILES
DESTS = X * ZP * Y
OWNERS = X * Z
CLASSES = ((0, 2, 4, 6), (1, 3, 5, 6))
USED = ((0, 2, 4), (1, 3, 5, 6))
DEPTH = 4
AXES = ("x", "zl", "zp", "core", "y")


def wanted(cls):
    return [
        (a, a + d) for a in range(SLOTS) for d in USED[cls] if a != MID and a + d != MID and a + d < SLOTS
    ]


WANTED = (wanted(0), wanted(1))
COUNT = max(len(w) for w in WANTED)


def runs(cls):
    out = {}
    for place, (a, s) in enumerate(WANTED[cls]):
        j = CLASSES[cls].index(s - a)
        mine = out.setdefault(a, [])
        if mine and mine[-1][0] + mine[-1][1] == j:
            mine[-1][1] += 1
        else:
            mine.append([j, 1, place])
    return list(out.items())


SMEM = pl.BlockSpec(memory_space=pltpu.SMEM)
ANY = pl.BlockSpec(memory_space=pl.ANY)
VMEM = pl.BlockSpec(memory_space=pltpu.VMEM)
MIB = 1 << 20


def near(value):
    return pltpu.with_memory_space_constraint(value, pltpu.VMEM)


def pack_kernel(values, out, stage, sems, out_sems):
    y = lax.axis_index("y")
    copies = []
    for x in range(X):
        for zp in range(ZP):
            for j, d in enumerate(CLASSES[zp]):
                rows = pl.ds(pl.multiple_of((x * Y + y) * TILE, TILE), TILE)
                n = len(copies)
                copies.append(
                    pltpu.make_async_copy(values.at[:, MID + d, rows], stage.at[x, zp, :, j], sems.at[n])
                )
    for copy in copies:
        copy.start()
    for copy in copies:
        copy.wait()
    copies = [pltpu.make_async_copy(stage, out.at[:, zl], out_sems.at[zl]) for zl in range(ZL)]
    for copy in copies:
        copy.start()
    for copy in copies:
        copy.wait()


def pack(values):
    shape = (X, ZP, ROWS_HERE, DEPTH, TILE, BLK)
    return pl.pallas_call(
        pack_kernel,
        out_shape=pltpu.VMEM((X, ZL) + shape[1:], jnp.bfloat16),
        in_specs=[ANY],
        out_specs=VMEM,
        scratch_shapes=[
            pltpu.VMEM(shape, jnp.bfloat16),
            pltpu.SemaphoreType.DMA((X * ZP * DEPTH,)),
            pltpu.SemaphoreType.DMA((ZL,)),
        ],
        compiler_params=pltpu.CompilerParams(vmem_limit_bytes=4 * MIB),
        name="pack",
    )(pltpu.with_memory_space_constraint(values, pltpu.HBM))


def select_kernel(lists, here, there, out, held, sems):
    zl, zp, core = (lax.axis_index(a) for a in ("zl", "zp", "core"))
    copies = [
        pltpu.make_async_copy(here, held.at[:, core], sems.at[0]),
        pltpu.make_async_copy(there, held.at[:, 1 - core], sems.at[1]),
    ]
    for copy in copies:
        copy.start()
    for copy in copies:
        copy.wait()

    rows = held.reshape(OWNERS * CORE * ROWS_HERE, DEPTH, TILE, BLK)

    def run(cls):
        def one(t, carry):
            owner = ((t // (ZP * Y)) * Z + 2 * zl + lax.rem(t // Y, ZP)) * CORE + core
            row = ROWS_HERE * owner + lax.rem(t, Y)
            for a, parts in runs(cls):
                k = jnp.maximum(lists[a, row], 0)
                for j, length, place in parts:
                    out[t, place : place + length] = rows[k, j : j + length]
            return carry

        lax.fori_loop(0, DESTS, one, 0)

    pl.when(zp == 0)(lambda: run(0))
    pl.when(zp == 1)(lambda: run(1))


def select(lists, here, there):
    return pl.pallas_call(
        select_kernel,
        out_shape=pltpu.VMEM((DESTS, COUNT, TILE, BLK), jnp.bfloat16),
        in_specs=[SMEM, VMEM, VMEM],
        out_specs=VMEM,
        scratch_shapes=[
            pltpu.VMEM((OWNERS, CORE, ROWS_HERE, DEPTH, TILE, BLK), jnp.bfloat16),
            pltpu.SemaphoreType.DMA((2,)),
        ],
        compiler_params=pltpu.CompilerParams(vmem_limit_bytes=12 * MIB),
        name="select",
    )(lists, near(here), near(there))


def groups():
    out = []
    for s in range(0, SLOTS, 2):
        n = min(2, SLOTS - s)
        low = max(0, s - MID)
        high = min(SLOTS - 1, s + n - 1 + MID)
        out.append((s, n, low, high - low + 1))
    return out


GROUPS = groups()


def purify_kernel(lists, got, own, out, u, w, sq, sems):
    x, zl, zp, core, y = (lax.axis_index(a) for a in AXES)
    row = ROWS_HERE * ((x * Z + 2 * zl + zp) * CORE + core) + y
    copies = []
    for p in range(DESTS):
        tile = (p // (ZP * Y)) * Y + p % Y
        copies.append(pltpu.make_async_copy(got.at[p], u.at[(p // Y) % ZP, :, tile], sems.at[p]))
    for s in range(SLOTS):
        copies.append(
            pltpu.make_async_copy(
                own.at[y, s],
                w.at[MID * BLK : (MID + 1) * BLK, s * BLK : (s + 1) * BLK],
                sems.at[DESTS + s],
            )
        )
    for copy in copies:
        copy.start()

    def blk(a):
        return slice(a * BLK, (a + 1) * BLK)

    for a in range(SLOTS - HALF):
        w[blk(a), blk(a + HALF)] = jnp.zeros((BLK, BLK), jnp.bfloat16)
        w[blk(a + HALF), blk(a)] = jnp.zeros((BLK, BLK), jnp.bfloat16)
    for copy in copies:
        copy.wait()
    for s in range(SLOTS):
        if s != MID:
            w[blk(s), blk(MID)] = w[blk(MID), blk(s)].T
    for cls in range(ZP):
        for place, (a, s) in enumerate(WANTED[cls]):
            value = u[cls, place].reshape(BLK, BLK)
            w[blk(a), blk(s)] = value
            if a != s:
                w[blk(s), blk(a)] = value.T

    def mask(value, s):
        return jnp.where(lists[s, row] >= 0, value, jnp.zeros_like(value))

    def span(first, n):
        return slice(first * BLK, (first + n) * BLK)

    for s, n, low, count in GROUPS:
        total = jnp.dot(
            w[blk(MID), span(low, count)], w[span(low, count), span(s, n)], preferred_element_type=jnp.float32
        )
        for j in range(n):
            sq[:, blk(s + j)] = mask(total[:, blk(j)], s + j).astype(jnp.bfloat16)
    for s, n, low, count in GROUPS:
        total = jnp.dot(sq[:, span(low, count)], w[span(low, count), span(s, n)], preferred_element_type=jnp.float32)
        for j in range(n):
            value = 3.0 * sq[:, blk(s + j)].astype(jnp.float32) - 2.0 * total[:, blk(j)]
            value = mask(value, s + j).T.astype(jnp.bfloat16)
            for part in range(Y):
                out[part, s + j] = value[part * (BLK // Y) : (part + 1) * (BLK // Y)]


def purify(lists, got, own):
    return pl.pallas_call(
        purify_kernel,
        out_shape=pltpu.VMEM((Y, SLOTS, BLK // Y, BLK), jnp.bfloat16),
        in_specs=[SMEM, VMEM, ANY],
        out_specs=VMEM,
        scratch_shapes=[
            pltpu.VMEM((ZP, COUNT, TILES, TILE, BLK), jnp.bfloat16),
            pltpu.VMEM((SLOTS * BLK, SLOTS * BLK), jnp.bfloat16),
            pltpu.VMEM((BLK, SLOTS * BLK), jnp.bfloat16),
            pltpu.SemaphoreType.DMA((DESTS + SLOTS,)),
        ],
        compiler_params=pltpu.CompilerParams(vmem_limit_bytes=24 * MIB),
        name="purify",
    )(lists, near(got), own)


def body(column_lists, block_values):
    lists = column_lists.T
    mine = pack(block_values).reshape(OWNERS, ROWS_HERE, DEPTH, TILE, BLK)
    here = lax.all_to_all(mine, ("x", "zl", "zp"), 0, 0, tiled=True)
    there = lax.ppermute(here, "core", [(0, 1), (1, 0)])
    asked = select(lists, here, there)
    got = lax.all_to_all(asked, ("x", "zp", "y"), 0, 0, tiled=True)
    strips = purify(lists, got, block_values)
    mixed = lax.all_to_all(strips, "y", 0, 0, tiled=True)
    return mixed.transpose(0, 1, 3, 2)


def solution(mesh):
    fine = Mesh(mesh.devices.reshape(X, ZL, ZP, CORE, Y), AXES)
    rows = ("x", "zl", "zp", "core")
    return jax.shard_map(
        body, mesh=fine, in_specs=(P(), P(rows)), out_specs=P(rows, None, None, "y"), check_vma=False
    )
```

```python
import jax
import jax.numpy as jnp
from jax import lax
from jax.experimental import pallas as pl
from jax.experimental.pallas import tpu as pltpu
from jax.sharding import Mesh
from jax.sharding import PartitionSpec as P

X, ZL, ZP, CORE, Y = 4, 4, 2, 2, 4
Z = ZL * ZP
BLK = 128
SLOTS = 13
MID = 6
HALF = 7
ROWS_HERE = 4
TILES = X * Y
TILE = BLK // TILES
DESTS = X * ZP * Y
OWNERS = X * Z
CLASSES = ((1, 4, 6), (2, 3, 5))
DEPTH = 3
FULL = DEPTH * ROWS_HERE
MESSAGE = FULL + ROWS_HERE // 2
AXES = ("x", "zl", "zp", "core", "y")


def wanted(cls):
    return [
        (a, a + d) for a in range(SLOTS) for d in CLASSES[cls] if a != MID and a + d != MID and a + d < SLOTS
    ]


WANTED = (wanted(0), wanted(1))
DIAGONAL = [a for a in range(SLOTS) if a != MID]
BASE = max(len(w) for w in WANTED)
COUNT = BASE + len(DIAGONAL) // 2
LANES = BLK // 2


def turned(value):
    return jnp.concatenate([value[:, LANES:], value[:, :LANES]], axis=1)


def joined(left, right):
    lane = lax.broadcasted_iota(jnp.int32, left.shape, 1)
    return jnp.where(lane < LANES, left, right)


SMEM = pl.BlockSpec(memory_space=pltpu.SMEM)
ANY = pl.BlockSpec(memory_space=pl.ANY)
VMEM = pl.BlockSpec(memory_space=pltpu.VMEM)
MIB = 1 << 20


def near(value):
    return pltpu.with_memory_space_constraint(value, pltpu.VMEM)


def pack_kernel(values, out, stage, diagonal, sems, out_sems):
    y = lax.axis_index("y")
    copies = []
    for x in range(X):
        rows = pl.ds(pl.multiple_of((x * Y + y) * TILE, TILE), TILE)
        targets = [(0, diagonal.at[x])]
        for zp in range(ZP):
            for j, d in enumerate(CLASSES[zp]):
                targets.append((d, stage.at[x, zp, j * ROWS_HERE : (j + 1) * ROWS_HERE]))
        for d, target in targets:
            copies.append(pltpu.make_async_copy(values.at[:, MID + d, rows], target, sems.at[len(copies)]))
    for copy in copies:
        copy.start()
    for copy in copies:
        copy.wait()
    for x in range(X):
        for m in range(ROWS_HERE // 2):
            one, two = diagonal[x, 2 * m], diagonal[x, 2 * m + 1]
            stage[x, 0, FULL + m] = joined(one, turned(two))
            stage[x, 1, FULL + m] = joined(turned(one), two)
    copies = [pltpu.make_async_copy(stage, out.at[:, zl], out_sems.at[zl]) for zl in range(ZL)]
    for copy in copies:
        copy.start()
    for copy in copies:
        copy.wait()


def pack(values):
    shape = (X, ZP, MESSAGE, TILE, BLK)
    return pl.pallas_call(
        pack_kernel,
        out_shape=pltpu.VMEM((X, ZL) + shape[1:], jnp.bfloat16),
        in_specs=[ANY],
        out_specs=VMEM,
        scratch_shapes=[
            pltpu.VMEM(shape, jnp.bfloat16),
            pltpu.VMEM((X, ROWS_HERE, TILE, BLK), jnp.bfloat16),
            pltpu.SemaphoreType.DMA((X * (1 + ZP * DEPTH),)),
            pltpu.SemaphoreType.DMA((ZL,)),
        ],
        compiler_params=pltpu.CompilerParams(vmem_limit_bytes=4 * MIB),
        name="pack",
    )(pltpu.with_memory_space_constraint(values, pltpu.HBM))


def select_kernel(lists, here, there, out, held, halves, sems):
    zl, zp, core = (lax.axis_index(a) for a in ("zl", "zp", "core"))
    copies = []
    for source, c in ((here, core), (there, 1 - core)):
        for part, target in ((source.at[:, :FULL], held.at[:, c]), (source.at[:, FULL:], halves.at[:, c])):
            copies.append(pltpu.make_async_copy(part, target, sems.at[len(copies)]))
    for copy in copies:
        copy.start()
    for copy in copies:
        copy.wait()
    rows = held.reshape(OWNERS * CORE * FULL, TILE, BLK)
    pairs = halves.reshape(OWNERS * CORE * ROWS_HERE // 2, TILE, BLK)

    def run(cls):
        def one(t, carry):
            owner = ((t // (ZP * Y)) * Z + 2 * zl + lax.rem(t // Y, ZP)) * CORE + core
            row = ROWS_HERE * owner + lax.rem(t, Y)
            target = {a: jnp.maximum(lists[a, row], 0) for a in DIAGONAL}
            first = {a: k + (k // ROWS_HERE) * (FULL - ROWS_HERE) for a, k in target.items()}
            for place, (a, s) in enumerate(WANTED[cls]):
                out[t, place] = rows[first[a] + ROWS_HERE * CLASSES[cls].index(s - a)]
            for p in range(len(DIAGONAL) // 2):
                k1, k2 = target[DIAGONAL[2 * p]], target[DIAGONAL[2 * p + 1]]
                one_half, two_half = pairs[k1 // 2], pairs[k2 // 2]
                left = jnp.where(lax.rem(k1, 2) == 1, turned(one_half), one_half)
                right = jnp.where(lax.rem(k2, 2) == 1, two_half, turned(two_half))
                out[t, BASE + p] = joined(left, right)
            return carry

        lax.fori_loop(0, DESTS, one, 0)

    pl.when(zp == 0)(lambda: run(0))
    pl.when(zp == 1)(lambda: run(1))


def select(lists, here, there):
    return pl.pallas_call(
        select_kernel,
        out_shape=pltpu.VMEM((DESTS, COUNT, TILE, BLK), jnp.bfloat16),
        in_specs=[SMEM, VMEM, VMEM],
        out_specs=VMEM,
        scratch_shapes=[
            pltpu.VMEM((OWNERS, CORE, FULL, TILE, BLK), jnp.bfloat16),
            pltpu.VMEM((OWNERS, CORE, ROWS_HERE // 2, TILE, BLK), jnp.bfloat16),
            pltpu.SemaphoreType.DMA((2 * CORE,)),
        ],
        compiler_params=pltpu.CompilerParams(vmem_limit_bytes=12 * MIB),
        name="select",
    )(lists, near(here), near(there))


def groups():
    out = []
    for s in range(0, SLOTS, 2):
        n = min(2, SLOTS - s)
        low = max(0, s - MID)
        high = min(SLOTS - 1, s + n - 1 + MID)
        out.append((s, n, low, high - low + 1))
    return out


GROUPS = groups()


def purify_kernel(lists, got, own, out, u, w, sq, sems):
    x, zl, zp, core, y = (lax.axis_index(a) for a in AXES)
    row = ROWS_HERE * ((x * Z + 2 * zl + zp) * CORE + core) + y
    copies = []
    for p in range(DESTS):
        tile = (p // (ZP * Y)) * Y + p % Y
        copies.append(pltpu.make_async_copy(got.at[p], u.at[(p // Y) % ZP, :, tile], sems.at[p]))
    for s in range(SLOTS):
        copies.append(
            pltpu.make_async_copy(
                own.at[y, s],
                w.at[MID * BLK : (MID + 1) * BLK, s * BLK : (s + 1) * BLK],
                sems.at[DESTS + s],
            )
        )
    for copy in copies:
        copy.start()

    def blk(a):
        return slice(a * BLK, (a + 1) * BLK)

    for a in range(SLOTS - HALF):
        w[blk(a), blk(a + HALF)] = jnp.zeros((BLK, BLK), jnp.bfloat16)
        w[blk(a + HALF), blk(a)] = jnp.zeros((BLK, BLK), jnp.bfloat16)
    for copy in copies:
        copy.wait()
    for s in range(SLOTS):
        if s != MID:
            w[blk(s), blk(MID)] = w[blk(MID), blk(s)].T
    for cls in range(ZP):
        for place, (a, s) in enumerate(WANTED[cls]):
            value = u[cls, place].reshape(BLK, BLK)
            w[blk(a), blk(s)] = value
            w[blk(s), blk(a)] = value.T
    for p in range(len(DIAGONAL) // 2):
        left, right = (u[cls, BASE + p].reshape(BLK, BLK) for cls in range(ZP))
        a, s = DIAGONAL[2 * p], DIAGONAL[2 * p + 1]
        w[blk(a), blk(a)] = joined(left, turned(right))
        w[blk(s), blk(s)] = joined(turned(left), right)

    def mask(value, s):
        return jnp.where(lists[s, row] >= 0, value, jnp.zeros_like(value))

    def span(first, n):
        return slice(first * BLK, (first + n) * BLK)

    for s, n, low, count in GROUPS:
        total = jnp.dot(
            w[blk(MID), span(low, count)], w[span(low, count), span(s, n)], preferred_element_type=jnp.float32
        )
        for j in range(n):
            sq[:, blk(s + j)] = mask(total[:, blk(j)], s + j).astype(jnp.bfloat16)
    for s, n, low, count in GROUPS:
        total = jnp.dot(sq[:, span(low, count)], w[span(low, count), span(s, n)], preferred_element_type=jnp.float32)
        for j in range(n):
            value = 3.0 * sq[:, blk(s + j)].astype(jnp.float32) - 2.0 * total[:, blk(j)]
            value = mask(value, s + j).T.astype(jnp.bfloat16)
            for part in range(Y):
                out[part, s + j] = value[part * (BLK // Y) : (part + 1) * (BLK // Y)]


def purify(lists, got, own):
    return pl.pallas_call(
        purify_kernel,
        out_shape=pltpu.VMEM((Y, SLOTS, BLK // Y, BLK), jnp.bfloat16),
        in_specs=[SMEM, VMEM, ANY],
        out_specs=VMEM,
        scratch_shapes=[
            pltpu.VMEM((ZP, COUNT, TILES, TILE, BLK), jnp.bfloat16),
            pltpu.VMEM((SLOTS * BLK, SLOTS * BLK), jnp.bfloat16),
            pltpu.VMEM((BLK, SLOTS * BLK), jnp.bfloat16),
            pltpu.SemaphoreType.DMA((DESTS + SLOTS,)),
        ],
        compiler_params=pltpu.CompilerParams(vmem_limit_bytes=24 * MIB),
        name="purify",
    )(lists, near(got), own)


def body(column_lists, block_values):
    lists = column_lists.T
    mine = pack(block_values).reshape(OWNERS, MESSAGE, TILE, BLK)
    here = lax.all_to_all(mine, ("x", "zl", "zp"), 0, 0, tiled=True)
    there = lax.ppermute(here, "core", [(0, 1), (1, 0)])
    asked = select(lists, here, there)
    got = lax.all_to_all(asked, ("x", "zp", "y"), 0, 0, tiled=True)
    strips = purify(lists, got, block_values)
    mixed = lax.all_to_all(strips, "y", 0, 0, tiled=True)
    return mixed.transpose(0, 1, 3, 2)


def solution(mesh):
    fine = Mesh(mesh.devices.reshape(X, ZL, ZP, CORE, Y), AXES)
    rows = ("x", "zl", "zp", "core")
    return jax.shard_map(
        body, mesh=fine, in_specs=(P(), P(rows)), out_specs=P(rows, None, None, "y"), check_vma=False
    )
```

```python
import jax
import jax.numpy as jnp
from jax import lax
from jax.experimental import pallas as pl
from jax.experimental.pallas import tpu as pltpu
from jax.sharding import Mesh
from jax.sharding import PartitionSpec as P

X, ZL, ZP, CORE, Y = 4, 4, 2, 2, 4
Z = ZL * ZP
BLK = 128
SLOTS = 13
MID = 6
HALF = 7
ROWS_HERE = 4
TILES = X * Y
TILE = BLK // TILES
DESTS = X * ZP * Y
OWNERS = X * Z
CLASSES = ((1, 4, 6), (2, 3, 5))
DEPTH = 3
FULL = DEPTH * ROWS_HERE
MESSAGE = FULL + ROWS_HERE // 2
AXES = ("x", "zl", "zp", "core", "y")


def wanted(cls):
    return [
        (a, a + d) for a in range(SLOTS) for d in CLASSES[cls] if a != MID and a + d != MID and a + d < SLOTS
    ]


WANTED = (wanted(0), wanted(1))
DIAGONAL = [a for a in range(SLOTS) if a != MID]
BASE = max(len(w) for w in WANTED)
COUNT = BASE + len(DIAGONAL) // 2
LANES = BLK // 2
PAIRS = OWNERS * CORE * ROWS_HERE // 2


def turned(value):
    return jnp.concatenate([value[:, LANES:], value[:, :LANES]], axis=1)


def joined(left, right):
    lane = lax.broadcasted_iota(jnp.int32, left.shape, 1)
    return jnp.where(lane < LANES, left, right)


SMEM = pl.BlockSpec(memory_space=pltpu.SMEM)
ANY = pl.BlockSpec(memory_space=pl.ANY)
VMEM = pl.BlockSpec(memory_space=pltpu.VMEM)
MIB = 1 << 20


def near(value):
    return pltpu.with_memory_space_constraint(value, pltpu.VMEM)


def pack_kernel(values, out, stage, diagonal, sems, out_sems):
    y = lax.axis_index("y")
    copies = []
    for x in range(X):
        rows = pl.ds(pl.multiple_of((x * Y + y) * TILE, TILE), TILE)
        targets = [(0, diagonal.at[x])]
        for zp in range(ZP):
            for j, d in enumerate(CLASSES[zp]):
                targets.append((d, stage.at[x, zp, j * ROWS_HERE : (j + 1) * ROWS_HERE]))
        for d, target in targets:
            copies.append(pltpu.make_async_copy(values.at[:, MID + d, rows], target, sems.at[len(copies)]))
    for copy in copies:
        copy.start()
    for copy in copies:
        copy.wait()
    for x in range(X):
        for m in range(ROWS_HERE // 2):
            one, two = diagonal[x, 2 * m], diagonal[x, 2 * m + 1]
            stage[x, 0, FULL + m] = joined(one, turned(two))
            stage[x, 1, FULL + m] = joined(turned(one), two)
    copies = [pltpu.make_async_copy(stage, out.at[:, zl], out_sems.at[zl]) for zl in range(ZL)]
    for copy in copies:
        copy.start()
    for copy in copies:
        copy.wait()


def pack(values):
    shape = (X, ZP, MESSAGE, TILE, BLK)
    return pl.pallas_call(
        pack_kernel,
        out_shape=pltpu.VMEM((X, ZL) + shape[1:], jnp.bfloat16),
        in_specs=[ANY],
        out_specs=VMEM,
        scratch_shapes=[
            pltpu.VMEM(shape, jnp.bfloat16),
            pltpu.VMEM((X, ROWS_HERE, TILE, BLK), jnp.bfloat16),
            pltpu.SemaphoreType.DMA((X * (1 + ZP * DEPTH),)),
            pltpu.SemaphoreType.DMA((ZL,)),
        ],
        compiler_params=pltpu.CompilerParams(vmem_limit_bytes=4 * MIB),
        name="pack",
    )(pltpu.with_memory_space_constraint(values, pltpu.HBM))


def select_kernel(lists, here, there, out, held, came, halves, sems):
    zl, zp, core = (lax.axis_index(a) for a in ("zl", "zp", "core"))
    copies = []
    for source, c in ((here, core), (there, 1 - core)):
        for j in range(DEPTH):
            part = source.at[:, j * ROWS_HERE : (j + 1) * ROWS_HERE]
            copies.append(pltpu.make_async_copy(part, held.at[j, :, c], sems.at[len(copies)]))
        copies.append(pltpu.make_async_copy(source.at[:, FULL:], came.at[:, c], sems.at[len(copies)]))
    for copy in copies:
        copy.start()
    for copy in copies:
        copy.wait()
    rows = held.reshape(DEPTH, OWNERS * CORE * ROWS_HERE, TILE, BLK)
    pairs = came.reshape(PAIRS, TILE, BLK)
    step = 16
    for n in range(0, PAIRS, step):
        value = pairs[n : n + step]
        halves[n : n + step, 0] = value
        halves[n : n + step, 1] = turned(value.reshape(step * TILE, BLK)).reshape(step, TILE, BLK)
    half = halves.reshape(2 * PAIRS, TILE, BLK)

    def run(cls):
        def one(t, carry):
            owner = (((t >> 3) * Z + 2 * zl + ((t >> 2) & 1)) << 1) + core
            row = (owner << 2) + (t & 3)
            target = {a: jnp.maximum(lists[a, row], 0) for a in DIAGONAL}
            for place, (a, s) in enumerate(WANTED[cls]):
                out[t, place] = rows[CLASSES[cls].index(s - a), target[a]]
            for p in range(len(DIAGONAL) // 2):
                left, right = half[target[DIAGONAL[2 * p]]], half[target[DIAGONAL[2 * p + 1]] ^ 1]
                out[t, BASE + p] = joined(left, right)
            return carry

        lax.fori_loop(0, DESTS, one, 0)

    pl.when(zp == 0)(lambda: run(0))
    pl.when(zp == 1)(lambda: run(1))


def select(lists, here, there):
    return pl.pallas_call(
        select_kernel,
        out_shape=pltpu.VMEM((DESTS, COUNT, TILE, BLK), jnp.bfloat16),
        in_specs=[SMEM, VMEM, VMEM],
        out_specs=VMEM,
        scratch_shapes=[
            pltpu.VMEM((DEPTH, OWNERS, CORE, ROWS_HERE, TILE, BLK), jnp.bfloat16),
            pltpu.VMEM((OWNERS, CORE, ROWS_HERE // 2, TILE, BLK), jnp.bfloat16),
            pltpu.VMEM((PAIRS, 2, TILE, BLK), jnp.bfloat16),
            pltpu.SemaphoreType.DMA((CORE * (DEPTH + 1),)),
        ],
        compiler_params=pltpu.CompilerParams(vmem_limit_bytes=12 * MIB),
        name="select",
    )(lists, near(here), near(there))


def groups():
    out = []
    for s in range(0, SLOTS, 2):
        n = min(2, SLOTS - s)
        low = max(0, s - MID)
        high = min(SLOTS - 1, s + n - 1 + MID)
        out.append((s, n, low, high - low + 1))
    return out


GROUPS = groups()


def purify_kernel(lists, got, own, out, u, w, sq, sems):
    x, zl, zp, core, y = (lax.axis_index(a) for a in AXES)
    row = ROWS_HERE * ((x * Z + 2 * zl + zp) * CORE + core) + y
    copies = []
    for p in range(DESTS):
        tile = (p // (ZP * Y)) * Y + p % Y
        copies.append(pltpu.make_async_copy(got.at[p], u.at[(p // Y) % ZP, :, tile], sems.at[p]))
    for s in range(SLOTS):
        copies.append(
            pltpu.make_async_copy(
                own.at[y, s],
                w.at[MID * BLK : (MID + 1) * BLK, s * BLK : (s + 1) * BLK],
                sems.at[DESTS + s],
            )
        )
    for copy in copies:
        copy.start()

    def blk(a):
        return slice(a * BLK, (a + 1) * BLK)

    for a in range(SLOTS - HALF):
        w[blk(a), blk(a + HALF)] = jnp.zeros((BLK, BLK), jnp.bfloat16)
        w[blk(a + HALF), blk(a)] = jnp.zeros((BLK, BLK), jnp.bfloat16)
    for copy in copies:
        copy.wait()
    for s in range(SLOTS):
        if s != MID:
            w[blk(s), blk(MID)] = w[blk(MID), blk(s)].T
    for cls in range(ZP):
        for place, (a, s) in enumerate(WANTED[cls]):
            value = u[cls, place].reshape(BLK, BLK)
            w[blk(a), blk(s)] = value
            w[blk(s), blk(a)] = value.T
    for p in range(len(DIAGONAL) // 2):
        left, right = (u[cls, BASE + p].reshape(BLK, BLK) for cls in range(ZP))
        a, s = DIAGONAL[2 * p], DIAGONAL[2 * p + 1]
        w[blk(a), blk(a)] = joined(left, turned(right))
        w[blk(s), blk(s)] = joined(turned(left), right)

    def mask(value, s):
        return jnp.where(lists[s, row] >= 0, value, jnp.zeros_like(value))

    def span(first, n):
        return slice(first * BLK, (first + n) * BLK)

    for s, n, low, count in GROUPS:
        total = jnp.dot(
            w[blk(MID), span(low, count)], w[span(low, count), span(s, n)], preferred_element_type=jnp.float32
        )
        for j in range(n):
            sq[:, blk(s + j)] = mask(total[:, blk(j)], s + j).astype(jnp.bfloat16)
    for s, n, low, count in GROUPS:
        total = jnp.dot(sq[:, span(low, count)], w[span(low, count), span(s, n)], preferred_element_type=jnp.float32)
        for j in range(n):
            value = 3.0 * sq[:, blk(s + j)].astype(jnp.float32) - 2.0 * total[:, blk(j)]
            value = mask(value, s + j).T.astype(jnp.bfloat16)
            for part in range(Y):
                out[part, s + j] = value[part * (BLK // Y) : (part + 1) * (BLK // Y)]


def purify(lists, got, own):
    return pl.pallas_call(
        purify_kernel,
        out_shape=pltpu.VMEM((Y, SLOTS, BLK // Y, BLK), jnp.bfloat16),
        in_specs=[SMEM, VMEM, ANY],
        out_specs=VMEM,
        scratch_shapes=[
            pltpu.VMEM((ZP, COUNT, TILES, TILE, BLK), jnp.bfloat16),
            pltpu.VMEM((SLOTS * BLK, SLOTS * BLK), jnp.bfloat16),
            pltpu.VMEM((BLK, SLOTS * BLK), jnp.bfloat16),
            pltpu.SemaphoreType.DMA((DESTS + SLOTS,)),
        ],
        compiler_params=pltpu.CompilerParams(vmem_limit_bytes=24 * MIB),
        name="purify",
    )(lists, near(got), own)


def body(column_lists, block_values):
    lists = column_lists.T
    mine = pack(block_values).reshape(OWNERS, MESSAGE, TILE, BLK)
    here = lax.all_to_all(mine, ("x", "zl", "zp"), 0, 0, tiled=True)
    there = lax.ppermute(here, "core", [(0, 1), (1, 0)])
    asked = select(lists, here, there)
    got = lax.all_to_all(asked, ("x", "zp", "y"), 0, 0, tiled=True)
    strips = purify(lists, got, block_values)
    mixed = lax.all_to_all(strips, "y", 0, 0, tiled=True)
    return mixed.transpose(0, 1, 3, 2)


def solution(mesh):
    fine = Mesh(mesh.devices.reshape(X, ZL, ZP, CORE, Y), AXES)
    rows = ("x", "zl", "zp", "core")
    return jax.shard_map(
        body, mesh=fine, in_specs=(P(), P(rows)), out_specs=P(rows, None, None, "y"), check_vma=False
    )
```

```python
import jax
import jax.numpy as jnp
from jax import lax
from jax.experimental import pallas as pl
from jax.experimental.pallas import tpu as pltpu
from jax.sharding import Mesh
from jax.sharding import PartitionSpec as P

X, ZL, ZP, CORE, Y = 4, 4, 2, 2, 4
Z = ZL * ZP
BLK = 128
SLOTS = 13
MID = 6
HALF = 7
ROWS_HERE = 4
TILES = X * Y
TILE = BLK // TILES
DESTS = X * ZP * Y
OWNERS = X * Z
CLASSES = ((1, 4, 6), (2, 3, 5))
DEPTH = 3
FULL = DEPTH * ROWS_HERE
MESSAGE = FULL + ROWS_HERE // 2
AXES = ("x", "zl", "zp", "core", "y")


def wanted(cls):
    return [
        (a, a + d) for a in range(SLOTS) for d in CLASSES[cls] if a != MID and a + d != MID and a + d < SLOTS
    ]


WANTED = (wanted(0), wanted(1))
DIAGONAL = [a for a in range(SLOTS) if a != MID]
BASE = max(len(w) for w in WANTED)
COUNT = BASE + len(DIAGONAL) // 2
LANES = BLK // 2
PAIRS = OWNERS * CORE * ROWS_HERE // 2


def turned(value):
    return jnp.concatenate([value[:, LANES:], value[:, :LANES]], axis=1)


def joined(left, right):
    lane = lax.broadcasted_iota(jnp.int32, left.shape, 1)
    return jnp.where(lane < LANES, left, right)


SMEM = pl.BlockSpec(memory_space=pltpu.SMEM)
ANY = pl.BlockSpec(memory_space=pl.ANY)
VMEM = pl.BlockSpec(memory_space=pltpu.VMEM)
MIB = 1 << 20


def near(value):
    return pltpu.with_memory_space_constraint(value, pltpu.VMEM)


def pack_kernel(values, out, stage, diagonal, sems, out_sems):
    y = lax.axis_index("y")
    copies = []
    for x in range(X):
        rows = pl.ds(pl.multiple_of((x * Y + y) * TILE, TILE), TILE)
        targets = [(0, diagonal.at[x])]
        for zp in range(ZP):
            for j, d in enumerate(CLASSES[zp]):
                targets.append((d, stage.at[x, zp, j * ROWS_HERE : (j + 1) * ROWS_HERE]))
        for d, target in targets:
            copies.append(pltpu.make_async_copy(values.at[:, MID + d, rows], target, sems.at[len(copies)]))
    for copy in copies:
        copy.start()
    for copy in copies:
        copy.wait()
    for x in range(X):
        for m in range(ROWS_HERE // 2):
            one, two = diagonal[x, 2 * m], diagonal[x, 2 * m + 1]
            stage[x, 0, FULL + m] = joined(one, turned(two))
            stage[x, 1, FULL + m] = joined(turned(one), two)
    copies = [pltpu.make_async_copy(stage, out.at[:, zl], out_sems.at[zl]) for zl in range(ZL)]
    for copy in copies:
        copy.start()
    for copy in copies:
        copy.wait()


def pack(values):
    shape = (X, ZP, MESSAGE, TILE, BLK)
    return pl.pallas_call(
        pack_kernel,
        out_shape=pltpu.VMEM((X, ZL) + shape[1:], jnp.bfloat16),
        in_specs=[ANY],
        out_specs=VMEM,
        scratch_shapes=[
            pltpu.VMEM(shape, jnp.bfloat16),
            pltpu.VMEM((X, ROWS_HERE, TILE, BLK), jnp.bfloat16),
            pltpu.SemaphoreType.DMA((X * (1 + ZP * DEPTH),)),
            pltpu.SemaphoreType.DMA((ZL,)),
        ],
        compiler_params=pltpu.CompilerParams(vmem_limit_bytes=4 * MIB),
        name="pack",
    )(pltpu.with_memory_space_constraint(values, pltpu.HBM))


def select_kernel(lists, here, there, out, held, came, halves, sems):
    zl, zp, core = (lax.axis_index(a) for a in ("zl", "zp", "core"))
    copies = []
    for source, c in ((here, core), (there, 1 - core)):
        for j in range(DEPTH):
            part = source.at[:, j * ROWS_HERE : (j + 1) * ROWS_HERE]
            copies.append(pltpu.make_async_copy(part, held.at[j, :, c], sems.at[len(copies)]))
        copies.append(pltpu.make_async_copy(source.at[:, FULL:], came.at[:, c], sems.at[len(copies)]))
    for copy in copies:
        copy.start()
    for copy in copies:
        copy.wait()
    rows = held.reshape(DEPTH, OWNERS * CORE * ROWS_HERE, TILE, BLK)
    pairs = came.reshape(PAIRS, TILE, BLK)
    step = 16
    for n in range(0, PAIRS, step):
        value = pairs[n : n + step]
        halves[n : n + step, 0] = value
        halves[n : n + step, 1] = turned(value.reshape(step * TILE, BLK)).reshape(step, TILE, BLK)
    half = halves.reshape(2 * PAIRS, TILE, BLK)

    def run(cls):
        def one(t, carry):
            owner = (((t >> 3) * Z + 2 * zl + ((t >> 2) & 1)) << 1) + core
            row = (owner << 2) + (t & 3)
            target = {a: jnp.maximum(lists[a, row], 0) for a in DIAGONAL}
            for place, (a, s) in enumerate(WANTED[cls]):
                out[t, place] = rows[CLASSES[cls].index(s - a), target[a]]
            for p in range(len(DIAGONAL) // 2):
                left, right = half[target[DIAGONAL[2 * p]]], half[target[DIAGONAL[2 * p + 1]] ^ 1]
                out[t, BASE + p] = joined(left, right)
            return carry

        lax.fori_loop(0, DESTS, one, 0)

    pl.when(zp == 0)(lambda: run(0))
    pl.when(zp == 1)(lambda: run(1))


def select(lists, here, there):
    return pl.pallas_call(
        select_kernel,
        out_shape=pltpu.VMEM((DESTS, COUNT, TILE, BLK), jnp.bfloat16),
        in_specs=[SMEM, VMEM, VMEM],
        out_specs=VMEM,
        scratch_shapes=[
            pltpu.VMEM((DEPTH, OWNERS, CORE, ROWS_HERE, TILE, BLK), jnp.bfloat16),
            pltpu.VMEM((OWNERS, CORE, ROWS_HERE // 2, TILE, BLK), jnp.bfloat16),
            pltpu.VMEM((PAIRS, 2, TILE, BLK), jnp.bfloat16),
            pltpu.SemaphoreType.DMA((CORE * (DEPTH + 1),)),
        ],
        compiler_params=pltpu.CompilerParams(vmem_limit_bytes=12 * MIB),
        name="select",
    )(lists, near(here), near(there))


def groups():
    out = []
    for s in range(0, SLOTS, 2):
        n = min(2, SLOTS - s)
        low = max(0, s - MID)
        high = min(SLOTS - 1, s + n - 1 + MID)
        out.append((s, n, low, high - low + 1))
    return out


GROUPS = groups()


def purify_kernel(lists, got, own, out, w, sq):
    x, zl, zp, core, y = (lax.axis_index(a) for a in AXES)
    row = ROWS_HERE * ((x * Z + 2 * zl + zp) * CORE + core) + y

    def blk(a):
        return slice(a * BLK, (a + 1) * BLK)

    def sent(cls, place):
        tiles = [got[((t // Y) * ZP + cls) * Y + t % Y, place] for t in range(TILES)]
        return jnp.concatenate(tiles, axis=0)

    for a in range(SLOTS - HALF):
        w[blk(a), blk(a + HALF)] = jnp.zeros((BLK, BLK), jnp.bfloat16)
        w[blk(a + HALF), blk(a)] = jnp.zeros((BLK, BLK), jnp.bfloat16)
    for s in range(SLOTS):
        value = own[y, s]
        w[blk(MID), blk(s)] = value
        if s != MID:
            w[blk(s), blk(MID)] = value.T
    for cls in range(ZP):
        for place, (a, s) in enumerate(WANTED[cls]):
            value = sent(cls, place)
            w[blk(a), blk(s)] = value
            w[blk(s), blk(a)] = value.T
    for p in range(len(DIAGONAL) // 2):
        left, right = (sent(cls, BASE + p) for cls in range(ZP))
        a, s = DIAGONAL[2 * p], DIAGONAL[2 * p + 1]
        w[blk(a), blk(a)] = joined(left, turned(right))
        w[blk(s), blk(s)] = joined(turned(left), right)

    def mask(value, s):
        return jnp.where(lists[s, row] >= 0, value, jnp.zeros_like(value))

    def span(first, n):
        return slice(first * BLK, (first + n) * BLK)

    for s, n, low, count in GROUPS:
        total = jnp.dot(
            w[blk(MID), span(low, count)], w[span(low, count), span(s, n)], preferred_element_type=jnp.float32
        )
        for j in range(n):
            sq[:, blk(s + j)] = mask(total[:, blk(j)], s + j).astype(jnp.bfloat16)
    for s, n, low, count in GROUPS:
        total = jnp.dot(sq[:, span(low, count)], w[span(low, count), span(s, n)], preferred_element_type=jnp.float32)
        for j in range(n):
            value = 3.0 * sq[:, blk(s + j)].astype(jnp.float32) - 2.0 * total[:, blk(j)]
            value = mask(value, s + j).T.astype(jnp.bfloat16)
            for part in range(Y):
                out[part, s + j] = value[part * (BLK // Y) : (part + 1) * (BLK // Y)]


def purify(lists, got, own):
    return pl.pallas_call(
        purify_kernel,
        out_shape=pltpu.VMEM((Y, SLOTS, BLK // Y, BLK), jnp.bfloat16),
        in_specs=[SMEM, VMEM, VMEM],
        out_specs=VMEM,
        scratch_shapes=[
            pltpu.VMEM((SLOTS * BLK, SLOTS * BLK), jnp.bfloat16),
            pltpu.VMEM((BLK, SLOTS * BLK), jnp.bfloat16),
        ],
        compiler_params=pltpu.CompilerParams(vmem_limit_bytes=24 * MIB),
        name="purify",
    )(lists, near(got), near(own))


def body(column_lists, block_values):
    lists = column_lists.T
    mine = pack(block_values).reshape(OWNERS, MESSAGE, TILE, BLK)
    here = lax.all_to_all(mine, ("x", "zl", "zp"), 0, 0, tiled=True)
    there = lax.ppermute(here, "core", [(0, 1), (1, 0)])
    asked = select(lists, here, there)
    got = lax.all_to_all(asked, ("x", "zp", "y"), 0, 0, tiled=True)
    strips = purify(lists, got, block_values)
    mixed = lax.all_to_all(strips, "y", 0, 0, tiled=True)
    return mixed.transpose(0, 1, 3, 2)


def solution(mesh):
    fine = Mesh(mesh.devices.reshape(X, ZL, ZP, CORE, Y), AXES)
    rows = ("x", "zl", "zp", "core")
    return jax.shard_map(
        body, mesh=fine, in_specs=(P(), P(rows)), out_specs=P(rows, None, None, "y"), check_vma=False
    )
```

```python
import jax
import jax.numpy as jnp
from jax import lax
from jax.experimental import pallas as pl
from jax.experimental.pallas import tpu as pltpu
from jax.sharding import Mesh
from jax.sharding import PartitionSpec as P

X, ZL, ZP, CORE, Y = 4, 4, 2, 2, 4
Z = ZL * ZP
BLK = 128
SLOTS = 13
MID = 6
HALF = 7
ROWS_HERE = 4
TILES = X * Y
TILE = BLK // TILES
DESTS = X * ZP * Y
OWNERS = X * Z
CLASSES = ((1, 4, 6), (2, 3, 5))
DEPTH = 3
FULL = DEPTH * ROWS_HERE
MESSAGE = FULL + ROWS_HERE // 2
AXES = ("x", "zl", "zp", "core", "y")


def wanted(cls):
    return [
        (a, a + d) for a in range(SLOTS) for d in CLASSES[cls] if a != MID and a + d != MID and a + d < SLOTS
    ]


WANTED = (wanted(0), wanted(1))
DIAGONAL = [a for a in range(SLOTS) if a != MID]
BASE = max(len(w) for w in WANTED)
COUNT = BASE + len(DIAGONAL) // 2
LANES = BLK // 2
PAIRS = OWNERS * CORE * ROWS_HERE // 2


def turned(value):
    return jnp.concatenate([value[:, LANES:], value[:, :LANES]], axis=1)


def joined(left, right):
    lane = lax.broadcasted_iota(jnp.int32, left.shape, 1)
    return jnp.where(lane < LANES, left, right)


SMEM = pl.BlockSpec(memory_space=pltpu.SMEM)
ANY = pl.BlockSpec(memory_space=pl.ANY)
VMEM = pl.BlockSpec(memory_space=pltpu.VMEM)
MIB = 1 << 20


def near(value):
    return pltpu.with_memory_space_constraint(value, pltpu.VMEM)


def pack_kernel(values, out, stage, diagonal, sems, out_sems):
    y = lax.axis_index("y")
    copies = []
    for x in range(X):
        rows = pl.ds(pl.multiple_of((x * Y + y) * TILE, TILE), TILE)
        targets = [(0, diagonal.at[x])]
        for zp in range(ZP):
            for j, d in enumerate(CLASSES[zp]):
                targets.append((d, stage.at[x, zp, j * ROWS_HERE : (j + 1) * ROWS_HERE]))
        for d, target in targets:
            copies.append(pltpu.make_async_copy(values.at[:, MID + d, rows], target, sems.at[len(copies)]))
    for copy in copies:
        copy.start()
    for copy in copies:
        copy.wait()
    for x in range(X):
        for m in range(ROWS_HERE // 2):
            one, two = diagonal[x, 2 * m], diagonal[x, 2 * m + 1]
            stage[x, 0, FULL + m] = joined(one, turned(two))
            stage[x, 1, FULL + m] = joined(turned(one), two)
    copies = [pltpu.make_async_copy(stage, out.at[:, zl], out_sems.at[zl]) for zl in range(ZL)]
    for copy in copies:
        copy.start()
    for copy in copies:
        copy.wait()


def pack(values):
    shape = (X, ZP, MESSAGE, TILE, BLK)
    return pl.pallas_call(
        pack_kernel,
        out_shape=pltpu.VMEM((X, ZL) + shape[1:], jnp.bfloat16),
        in_specs=[ANY],
        out_specs=VMEM,
        scratch_shapes=[
            pltpu.VMEM(shape, jnp.bfloat16),
            pltpu.VMEM((X, ROWS_HERE, TILE, BLK), jnp.bfloat16),
            pltpu.SemaphoreType.DMA((X * (1 + ZP * DEPTH),)),
            pltpu.SemaphoreType.DMA((ZL,)),
        ],
        compiler_params=pltpu.CompilerParams(vmem_limit_bytes=4 * MIB),
        name="pack",
    )(pltpu.with_memory_space_constraint(values, pltpu.HBM))


def select_kernel(lists, here, there, out, held, came, halves, sems):
    zl, zp, core = (lax.axis_index(a) for a in ("zl", "zp", "core"))
    copies = []
    for source, c in ((here, core), (there, 1 - core)):
        for j in range(DEPTH):
            part = source.at[:, j * ROWS_HERE : (j + 1) * ROWS_HERE]
            copies.append(pltpu.make_async_copy(part, held.at[j, :, c], sems.at[len(copies)]))
        copies.append(pltpu.make_async_copy(source.at[:, FULL:], came.at[:, c], sems.at[len(copies)]))
    for copy in copies:
        copy.start()
    for copy in copies:
        copy.wait()
    rows = held.reshape(DEPTH, OWNERS * CORE * ROWS_HERE, TILE, BLK)
    pairs = came.reshape(PAIRS, TILE, BLK)
    step = 16
    for n in range(0, PAIRS, step):
        value = pairs[n : n + step]
        halves[n : n + step, 0] = value
        halves[n : n + step, 1] = turned(value.reshape(step * TILE, BLK)).reshape(step, TILE, BLK)
    half = halves.reshape(2 * PAIRS, TILE, BLK)

    def run(cls):
        def one(t, carry):
            owner = (((t >> 3) * Z + 2 * zl + ((t >> 2) & 1)) << 1) + core
            row = (owner << 2) + (t & 3)
            target = {a: jnp.maximum(lists[a, row], 0) for a in DIAGONAL}
            for place, (a, s) in enumerate(WANTED[cls]):
                out[t, place] = rows[CLASSES[cls].index(s - a), target[a]]
            for p in range(len(DIAGONAL) // 2):
                left, right = half[target[DIAGONAL[2 * p]]], half[target[DIAGONAL[2 * p + 1]] ^ 1]
                out[t, BASE + p] = joined(left, right)
            return carry

        lax.fori_loop(0, DESTS, one, 0)

    pl.when(zp == 0)(lambda: run(0))
    pl.when(zp == 1)(lambda: run(1))


def select(lists, here, there):
    return pl.pallas_call(
        select_kernel,
        out_shape=pltpu.VMEM((DESTS, COUNT, TILE, BLK), jnp.bfloat16),
        in_specs=[SMEM, VMEM, VMEM],
        out_specs=VMEM,
        scratch_shapes=[
            pltpu.VMEM((DEPTH, OWNERS, CORE, ROWS_HERE, TILE, BLK), jnp.bfloat16),
            pltpu.VMEM((OWNERS, CORE, ROWS_HERE // 2, TILE, BLK), jnp.bfloat16),
            pltpu.VMEM((PAIRS, 2, TILE, BLK), jnp.bfloat16),
            pltpu.SemaphoreType.DMA((CORE * (DEPTH + 1),)),
        ],
        compiler_params=pltpu.CompilerParams(vmem_limit_bytes=12 * MIB),
        name="select",
    )(lists, near(here), near(there))


def groups():
    out = []
    for s in range(0, SLOTS, 2):
        n = min(2, SLOTS - s)
        low = max(0, s - MID)
        high = min(SLOTS - 1, s + n - 1 + MID)
        out.append((s, n, low, high - low + 1))
    return out


GROUPS = groups()


def purify_kernel(lists, got, own, out, w, sq):
    x, zl, zp, core, y = (lax.axis_index(a) for a in AXES)
    row = ROWS_HERE * ((x * Z + 2 * zl + zp) * CORE + core) + y

    def blk(a):
        return slice(a * BLK, (a + 1) * BLK)

    def sent(cls, place):
        tiles = [got[((t // Y) * ZP + cls) * Y + t % Y, place] for t in range(TILES)]
        return jnp.concatenate(tiles, axis=0)

    for a in range(SLOTS - HALF):
        w[blk(a), blk(a + HALF)] = jnp.zeros((BLK, BLK), jnp.bfloat16)
        w[blk(a + HALF), blk(a)] = jnp.zeros((BLK, BLK), jnp.bfloat16)
    for s in range(SLOTS):
        value = own[y, s]
        w[blk(MID), blk(s)] = value
        if s != MID:
            w[blk(s), blk(MID)] = value.T
    for cls in range(ZP):
        for place, (a, s) in enumerate(WANTED[cls]):
            value = sent(cls, place)
            w[blk(a), blk(s)] = value
            w[blk(s), blk(a)] = value.T
    for p in range(len(DIAGONAL) // 2):
        left, right = (sent(cls, BASE + p) for cls in range(ZP))
        a, s = DIAGONAL[2 * p], DIAGONAL[2 * p + 1]
        w[blk(a), blk(a)] = joined(left, turned(right))
        w[blk(s), blk(s)] = joined(turned(left), right)

    def mask(value, s):
        return jnp.where(lists[s, row] >= 0, value, jnp.zeros_like(value))

    def span(first, n):
        return slice(first * BLK, (first + n) * BLK)

    for s, n, low, count in GROUPS:
        total = jnp.dot(
            w[blk(MID), span(low, count)], w[span(low, count), span(s, n)], preferred_element_type=jnp.float32
        )
        for j in range(n):
            sq[:, blk(s + j)] = mask(total[:, blk(j)], s + j).astype(jnp.bfloat16)
    for s, n, low, count in GROUPS:
        total = jnp.dot(sq[:, span(low, count)], w[span(low, count), span(s, n)], preferred_element_type=jnp.float32)
        for j in range(n):
            value = 3.0 * sq[:, blk(s + j)].astype(jnp.float32) - 2.0 * total[:, blk(j)]
            value = mask(value, s + j).T.astype(jnp.bfloat16)
            for part in range(Y):
                out[(part - y) & (Y - 1), s + j] = value[part * (BLK // Y) : (part + 1) * (BLK // Y)]


def purify(lists, got, own):
    return pl.pallas_call(
        purify_kernel,
        out_shape=pltpu.VMEM((Y, SLOTS, BLK // Y, BLK), jnp.bfloat16),
        in_specs=[SMEM, VMEM, VMEM],
        out_specs=VMEM,
        scratch_shapes=[
            pltpu.VMEM((SLOTS * BLK, SLOTS * BLK), jnp.bfloat16),
            pltpu.VMEM((BLK, SLOTS * BLK), jnp.bfloat16),
        ],
        compiler_params=pltpu.CompilerParams(vmem_limit_bytes=24 * MIB),
        name="purify",
    )(lists, near(got), near(own))


def place_kernel(own, one, two, three, out, sems):
    y = lax.axis_index("y")
    parts = (own.at[0], one, two, three)
    copies = [pltpu.make_async_copy(part, out.at[(y - n) & (Y - 1)], sems.at[n]) for n, part in enumerate(parts)]
    for copy in copies:
        copy.start()
    for copy in copies:
        copy.wait()


def place(strips, parts):
    return pl.pallas_call(
        place_kernel,
        out_shape=pltpu.HBM((Y, SLOTS, BLK // Y, BLK), jnp.bfloat16),
        in_specs=[VMEM] * Y,
        out_specs=pl.BlockSpec(memory_space=pltpu.HBM),
        scratch_shapes=[pltpu.SemaphoreType.DMA((Y,))],
        compiler_params=pltpu.CompilerParams(vmem_limit_bytes=4 * MIB),
        name="place",
    )(*(near(p) for p in (strips, *parts)))


def body(column_lists, block_values):
    lists = column_lists.T
    mine = pack(block_values).reshape(OWNERS, MESSAGE, TILE, BLK)
    here = lax.all_to_all(mine, ("x", "zl", "zp"), 0, 0, tiled=True)
    there = lax.ppermute(here, "core", [(0, 1), (1, 0)])
    asked = select(lists, here, there)
    got = lax.all_to_all(asked, ("x", "zp", "y"), 0, 0, tiled=True)
    strips = purify(lists, got, block_values)
    two, one, three = (
        lax.ppermute(strips[n], "y", [(i, (i + n) % Y) for i in range(Y)]) for n in (2, 1, 3)
    )
    mixed = place(strips, (one, two, three))
    return mixed.transpose(0, 1, 3, 2)


def solution(mesh):
    fine = Mesh(mesh.devices.reshape(X, ZL, ZP, CORE, Y), AXES)
    rows = ("x", "zl", "zp", "core")
    return jax.shard_map(
        body, mesh=fine, in_specs=(P(), P(rows)), out_specs=P(rows, None, None, "y"), check_vma=False
    )
```

```python
import jax
import jax.numpy as jnp
from jax import lax
from jax.experimental import pallas as pl
from jax.experimental.pallas import tpu as pltpu
from jax.sharding import Mesh
from jax.sharding import PartitionSpec as P

X, ZL, ZP, CORE, Y = 4, 4, 2, 2, 4
Z = ZL * ZP
BLK = 128
SLOTS = 13
MID = 6
HALF = 7
ROWS_HERE = 4
TILES = X * Y
TILE = BLK // TILES
DESTS = X * ZP * Y
OWNERS = X * Z
CLASSES = ((1, 4, 6), (2, 3, 5))
DEPTH = 3
FULL = DEPTH * ROWS_HERE
MESSAGE = FULL + ROWS_HERE // 2
AXES = ("x", "zl", "zp", "core", "y")


def wanted(cls):
    return [
        (a, a + d) for a in range(SLOTS) for d in CLASSES[cls] if a != MID and a + d != MID and a + d < SLOTS
    ]


WANTED = (wanted(0), wanted(1))
DIAGONAL = [a for a in range(SLOTS) if a != MID]
BASE = max(len(w) for w in WANTED)
COUNT = BASE + len(DIAGONAL) // 2
LANES = BLK // 2
PARTS = ((0, slice(0, X)), (1, slice(0, X)), (-1, slice(0, X)), (2, slice(0, X // 2)), (2, slice(X // 2, X)))
PAIRS = OWNERS * CORE * ROWS_HERE // 2


def turned(value):
    return jnp.concatenate([value[:, LANES:], value[:, :LANES]], axis=1)


def joined(left, right):
    lane = lax.broadcasted_iota(jnp.int32, left.shape, 1)
    return jnp.where(lane < LANES, left, right)


SMEM = pl.BlockSpec(memory_space=pltpu.SMEM)
ANY = pl.BlockSpec(memory_space=pl.ANY)
VMEM = pl.BlockSpec(memory_space=pltpu.VMEM)
MIB = 1 << 20


def near(value):
    return pltpu.with_memory_space_constraint(value, pltpu.VMEM)


def pack_kernel(values, out, diagonal, sems):
    y = lax.axis_index("y")
    copies = []
    for x in range(X):
        rows = pl.ds(pl.multiple_of((x * Y + y) * TILE, TILE), TILE)
        targets = [(0, diagonal.at[x])]
        for zp in range(ZP):
            for j, d in enumerate(CLASSES[zp]):
                targets.append((d, out.at[x, zp, j * ROWS_HERE : (j + 1) * ROWS_HERE]))
        for d, target in targets:
            copies.append(pltpu.make_async_copy(values.at[:, MID + d, rows], target, sems.at[len(copies)]))
    for copy in copies:
        copy.start()
    for copy in copies:
        copy.wait()
    for x in range(X):
        for m in range(ROWS_HERE // 2):
            one, two = diagonal[x, 2 * m], diagonal[x, 2 * m + 1]
            out[x, 0, FULL + m] = joined(one, turned(two))
            out[x, 1, FULL + m] = joined(turned(one), two)


def pack(values):
    return pl.pallas_call(
        pack_kernel,
        out_shape=pltpu.VMEM((X, ZP, MESSAGE, TILE, BLK), jnp.bfloat16),
        in_specs=[ANY],
        out_specs=VMEM,
        scratch_shapes=[
            pltpu.VMEM((X, ROWS_HERE, TILE, BLK), jnp.bfloat16),
            pltpu.SemaphoreType.DMA((X * (1 + ZP * DEPTH),)),
        ],
        compiler_params=pltpu.CompilerParams(vmem_limit_bytes=4 * MIB),
        name="pack",
    )(pltpu.with_memory_space_constraint(values, pltpu.HBM))


def select_kernel(lists, *refs):
    pieces, (out, held, came, halves, sems) = refs[: 2 * len(PARTS)], refs[2 * len(PARTS) :]
    zl, zp, core = (lax.axis_index(a) for a in ("zl", "zp", "core"))
    copies = []
    for n, source in enumerate(pieces):
        c = core if n < len(PARTS) else 1 - core
        step, xs = PARTS[n % len(PARTS)]
        there = (zl + step) & (ZL - 1)
        for j in range(DEPTH):
            part = source.at[:, :, j * ROWS_HERE : (j + 1) * ROWS_HERE]
            copies.append(pltpu.make_async_copy(part, held.at[j, xs, there, :, c], sems.at[len(copies)]))
        copies.append(pltpu.make_async_copy(source.at[:, :, FULL:], came.at[xs, there, :, c], sems.at[len(copies)]))
    for copy in copies:
        copy.start()
    for copy in copies:
        copy.wait()
    rows = held.reshape(DEPTH, OWNERS * CORE * ROWS_HERE, TILE, BLK)
    pairs = came.reshape(PAIRS, TILE, BLK)
    step = 16
    for n in range(0, PAIRS, step):
        value = pairs[n : n + step]
        halves[n : n + step, 0] = value
        halves[n : n + step, 1] = turned(value.reshape(step * TILE, BLK)).reshape(step, TILE, BLK)
    half = halves.reshape(2 * PAIRS, TILE, BLK)

    def run(cls):
        def one(t, carry):
            owner = (((t >> 3) * Z + 2 * zl + ((t >> 2) & 1)) << 1) + core
            row = (owner << 2) + (t & 3)
            target = {a: jnp.maximum(lists[a, row], 0) for a in DIAGONAL}
            for place, (a, s) in enumerate(WANTED[cls]):
                out[t, place] = rows[CLASSES[cls].index(s - a), target[a]]
            for p in range(len(DIAGONAL) // 2):
                left, right = half[target[DIAGONAL[2 * p]]], half[target[DIAGONAL[2 * p + 1]] ^ 1]
                out[t, BASE + p] = joined(left, right)
            return carry

        lax.fori_loop(0, DESTS, one, 0)

    pl.when(zp == 0)(lambda: run(0))
    pl.when(zp == 1)(lambda: run(1))


def select(lists, pieces):
    return pl.pallas_call(
        select_kernel,
        out_shape=pltpu.VMEM((DESTS, COUNT, TILE, BLK), jnp.bfloat16),
        in_specs=[SMEM] + [VMEM] * (2 * len(PARTS)),
        out_specs=VMEM,
        scratch_shapes=[
            pltpu.VMEM((DEPTH, X, ZL, ZP, CORE, ROWS_HERE, TILE, BLK), jnp.bfloat16),
            pltpu.VMEM((X, ZL, ZP, CORE, ROWS_HERE // 2, TILE, BLK), jnp.bfloat16),
            pltpu.VMEM((PAIRS, 2, TILE, BLK), jnp.bfloat16),
            pltpu.SemaphoreType.DMA((CORE * len(PARTS) * (DEPTH + 1),)),
        ],
        compiler_params=pltpu.CompilerParams(vmem_limit_bytes=12 * MIB),
        name="select",
    )(lists, *(near(p) for p in pieces))


def groups():
    out = []
    for s in range(0, SLOTS, 2):
        n = min(2, SLOTS - s)
        low = max(0, s - MID)
        high = min(SLOTS - 1, s + n - 1 + MID)
        out.append((s, n, low, high - low + 1))
    return out


GROUPS = groups()


def purify_kernel(lists, got, own, out, w, sq):
    x, zl, zp, core, y = (lax.axis_index(a) for a in AXES)
    row = ROWS_HERE * ((x * Z + 2 * zl + zp) * CORE + core) + y

    def blk(a):
        return slice(a * BLK, (a + 1) * BLK)

    def sent(cls, place):
        tiles = [got[((t // Y) * ZP + cls) * Y + t % Y, place] for t in range(TILES)]
        return jnp.concatenate(tiles, axis=0)

    for a in range(SLOTS - HALF):
        w[blk(a), blk(a + HALF)] = jnp.zeros((BLK, BLK), jnp.bfloat16)
        w[blk(a + HALF), blk(a)] = jnp.zeros((BLK, BLK), jnp.bfloat16)
    for s in range(SLOTS):
        value = own[y, s]
        w[blk(MID), blk(s)] = value
        if s != MID:
            w[blk(s), blk(MID)] = value.T
    for cls in range(ZP):
        for place, (a, s) in enumerate(WANTED[cls]):
            value = sent(cls, place)
            w[blk(a), blk(s)] = value
            w[blk(s), blk(a)] = value.T
    for p in range(len(DIAGONAL) // 2):
        left, right = (sent(cls, BASE + p) for cls in range(ZP))
        a, s = DIAGONAL[2 * p], DIAGONAL[2 * p + 1]
        w[blk(a), blk(a)] = joined(left, turned(right))
        w[blk(s), blk(s)] = joined(turned(left), right)

    def mask(value, s):
        return jnp.where(lists[s, row] >= 0, value, jnp.zeros_like(value))

    def span(first, n):
        return slice(first * BLK, (first + n) * BLK)

    for s, n, low, count in GROUPS:
        total = jnp.dot(
            w[blk(MID), span(low, count)], w[span(low, count), span(s, n)], preferred_element_type=jnp.float32
        )
        for j in range(n):
            sq[:, blk(s + j)] = mask(total[:, blk(j)], s + j).astype(jnp.bfloat16)
    for s, n, low, count in GROUPS:
        total = jnp.dot(sq[:, span(low, count)], w[span(low, count), span(s, n)], preferred_element_type=jnp.float32)
        for j in range(n):
            value = 3.0 * sq[:, blk(s + j)].astype(jnp.float32) - 2.0 * total[:, blk(j)]
            value = mask(value, s + j).T.astype(jnp.bfloat16)
            for part in range(Y):
                out[(part - y) & (Y - 1), s + j] = value[part * (BLK // Y) : (part + 1) * (BLK // Y)]


def purify(lists, got, own):
    return pl.pallas_call(
        purify_kernel,
        out_shape=pltpu.VMEM((Y, SLOTS, BLK // Y, BLK), jnp.bfloat16),
        in_specs=[SMEM, VMEM, VMEM],
        out_specs=VMEM,
        scratch_shapes=[
            pltpu.VMEM((SLOTS * BLK, SLOTS * BLK), jnp.bfloat16),
            pltpu.VMEM((BLK, SLOTS * BLK), jnp.bfloat16),
        ],
        compiler_params=pltpu.CompilerParams(vmem_limit_bytes=24 * MIB),
        name="purify",
    )(lists, near(got), near(own))


def place_kernel(own, one, two, three, out, sems):
    y = lax.axis_index("y")
    parts = (own.at[0], one, two, three)
    copies = [pltpu.make_async_copy(part, out.at[(y - n) & (Y - 1)], sems.at[n]) for n, part in enumerate(parts)]
    for copy in copies:
        copy.start()
    for copy in copies:
        copy.wait()


def place(strips, parts):
    return pl.pallas_call(
        place_kernel,
        out_shape=pltpu.HBM((Y, SLOTS, BLK // Y, BLK), jnp.bfloat16),
        in_specs=[VMEM] * Y,
        out_specs=pl.BlockSpec(memory_space=pltpu.HBM),
        scratch_shapes=[pltpu.SemaphoreType.DMA((Y,))],
        compiler_params=pltpu.CompilerParams(vmem_limit_bytes=4 * MIB),
        name="place",
    )(*(near(p) for p in (strips, *parts)))


def shifted(value, step):
    return lax.ppermute(value, "zl", [((i + step) % ZL, i) for i in range(ZL)])


def body(column_lists, block_values):
    lists = column_lists.T
    mine = pack(block_values).reshape(X * ZP, MESSAGE, TILE, BLK)
    part = lax.all_to_all(mine, ("x", "zp"), 0, 0, tiled=True).reshape(X, ZP, MESSAGE, TILE, BLK)
    ahead, behind = shifted(part, 1), shifted(part, -1)
    far = shifted(ahead[: X // 2], 1), shifted(behind[X // 2 :], -1)
    here = [part, ahead, behind, *far]
    near_pieces = lax.optimization_barrier((ahead, behind))
    there = [lax.ppermute(p, "core", [(0, 1), (1, 0)]) for p in (part, *near_pieces, *far)]
    asked = select(lists, here + there)
    got = lax.all_to_all(asked, ("x", "zp", "y"), 0, 0, tiled=True)
    strips = purify(lists, got, block_values)
    two, one, three = (
        lax.ppermute(strips[n], "y", [(i, (i + n) % Y) for i in range(Y)]) for n in (2, 1, 3)
    )
    mixed = place(strips, (one, two, three))
    return mixed.transpose(0, 1, 3, 2)


def solution(mesh):
    fine = Mesh(mesh.devices.reshape(X, ZL, ZP, CORE, Y), AXES)
    rows = ("x", "zl", "zp", "core")
    return jax.shard_map(
        body, mesh=fine, in_specs=(P(), P(rows)), out_specs=P(rows, None, None, "y"), check_vma=False
    )
```

```python
import jax
import jax.numpy as jnp
from jax import lax
from jax.experimental import pallas as pl
from jax.experimental.pallas import tpu as pltpu
from jax.sharding import Mesh
from jax.sharding import PartitionSpec as P

X, ZL, ZP, CORE, Y = 4, 4, 2, 2, 4
Z = ZL * ZP
BLK = 128
SLOTS = 13
MID = 6
HALF = 7
ROWS_HERE = 4
TILES = X * Y
TILE = BLK // TILES
DESTS = X * ZP * Y
OWNERS = X * Z
CLASSES = ((1, 4, 6), (2, 3, 5))
DEPTH = 3
FULL = DEPTH * ROWS_HERE
MESSAGE = FULL + ROWS_HERE // 2
AXES = ("x", "zl", "zp", "core", "y")


def wanted(cls):
    return [
        (a, a + d) for a in range(SLOTS) for d in CLASSES[cls] if a != MID and a + d != MID and a + d < SLOTS
    ]


WANTED = (wanted(0), wanted(1))
DIAGONAL = [a for a in range(SLOTS) if a != MID]
BASE = max(len(w) for w in WANTED)
COUNT = BASE + len(DIAGONAL) // 2
LANES = BLK // 2
PARTS = ((0, slice(0, X)), (1, slice(0, X)), (-1, slice(0, X)), (2, slice(0, X // 2)), (2, slice(X // 2, X)))
PAIRS = OWNERS * CORE * ROWS_HERE // 2


def turned(value):
    return jnp.concatenate([value[:, LANES:], value[:, :LANES]], axis=1)


def joined(left, right):
    lane = lax.broadcasted_iota(jnp.int32, left.shape, 1)
    return jnp.where(lane < LANES, left, right)


SMEM = pl.BlockSpec(memory_space=pltpu.SMEM)
ANY = pl.BlockSpec(memory_space=pl.ANY)
VMEM = pl.BlockSpec(memory_space=pltpu.VMEM)
MIB = 1 << 20


def near(value):
    return pltpu.with_memory_space_constraint(value, pltpu.VMEM)


def pack_kernel(values, out, diagonal, sems):
    y = lax.axis_index("y")
    copies = []
    for x in range(X):
        rows = pl.ds(pl.multiple_of((x * Y + y) * TILE, TILE), TILE)
        targets = [(0, diagonal.at[x])]
        for zp in range(ZP):
            for j, d in enumerate(CLASSES[zp]):
                targets.append((d, out.at[x, zp, j * ROWS_HERE : (j + 1) * ROWS_HERE]))
        for d, target in targets:
            copies.append(pltpu.make_async_copy(values.at[:, MID + d, rows], target, sems.at[len(copies)]))
    for copy in copies:
        copy.start()
    for copy in copies:
        copy.wait()
    for x in range(X):
        for m in range(ROWS_HERE // 2):
            one, two = diagonal[x, 2 * m], diagonal[x, 2 * m + 1]
            out[x, 0, FULL + m] = joined(one, turned(two))
            out[x, 1, FULL + m] = joined(turned(one), two)


def pack(values):
    return pl.pallas_call(
        pack_kernel,
        out_shape=pltpu.VMEM((X, ZP, MESSAGE, TILE, BLK), jnp.bfloat16),
        in_specs=[ANY],
        out_specs=VMEM,
        scratch_shapes=[
            pltpu.VMEM((X, ROWS_HERE, TILE, BLK), jnp.bfloat16),
            pltpu.SemaphoreType.DMA((X * (1 + ZP * DEPTH),)),
        ],
        compiler_params=pltpu.CompilerParams(vmem_limit_bytes=4 * MIB),
        name="pack",
    )(pltpu.with_memory_space_constraint(values, pltpu.HBM))


def select_kernel(lists, *refs):
    pieces, (out, held, came, halves, sems) = refs[: 2 * len(PARTS)], refs[2 * len(PARTS) :]
    zl, zp, core = (lax.axis_index(a) for a in ("zl", "zp", "core"))
    copies = []
    for n, source in enumerate(pieces):
        c = core if n < len(PARTS) else 1 - core
        step, xs = PARTS[n % len(PARTS)]
        there = (zl + step) & (ZL - 1)
        for j in range(DEPTH):
            part = source.at[:, :, j * ROWS_HERE : (j + 1) * ROWS_HERE]
            copies.append(pltpu.make_async_copy(part, held.at[j, xs, there, :, c], sems.at[len(copies)]))
        copies.append(pltpu.make_async_copy(source.at[:, :, FULL:], came.at[xs, there, :, c], sems.at[len(copies)]))
    for copy in copies:
        copy.start()
    for copy in copies:
        copy.wait()
    rows = held.reshape(DEPTH, OWNERS * CORE * ROWS_HERE, TILE, BLK)
    pairs = came.reshape(PAIRS, TILE, BLK)
    step = 16
    for n in range(0, PAIRS, step):
        value = pairs[n : n + step]
        halves[n : n + step, 0] = value
        halves[n : n + step, 1] = turned(value.reshape(step * TILE, BLK)).reshape(step, TILE, BLK)
    half = halves.reshape(2 * PAIRS, TILE, BLK)

    def run(cls):
        def one(t, carry):
            owner = (((t >> 3) * Z + 2 * zl + ((t >> 2) & 1)) << 1) + core
            row = (owner << 2) + (t & 3)
            target = {a: jnp.maximum(lists[a, row], 0) for a in DIAGONAL}
            for place, (a, s) in enumerate(WANTED[cls]):
                out[t, place] = rows[CLASSES[cls].index(s - a), target[a]]
            for p in range(len(DIAGONAL) // 2):
                left, right = half[target[DIAGONAL[2 * p]]], half[target[DIAGONAL[2 * p + 1]] ^ 1]
                out[t, BASE + p] = joined(left, right)
            return carry

        lax.fori_loop(0, DESTS, one, 0)

    pl.when(zp == 0)(lambda: run(0))
    pl.when(zp == 1)(lambda: run(1))


def select(lists, pieces):
    return pl.pallas_call(
        select_kernel,
        out_shape=pltpu.VMEM((DESTS, COUNT, TILE, BLK), jnp.bfloat16),
        in_specs=[SMEM] + [VMEM] * (2 * len(PARTS)),
        out_specs=VMEM,
        scratch_shapes=[
            pltpu.VMEM((DEPTH, X, ZL, ZP, CORE, ROWS_HERE, TILE, BLK), jnp.bfloat16),
            pltpu.VMEM((X, ZL, ZP, CORE, ROWS_HERE // 2, TILE, BLK), jnp.bfloat16),
            pltpu.VMEM((PAIRS, 2, TILE, BLK), jnp.bfloat16),
            pltpu.SemaphoreType.DMA((CORE * len(PARTS) * (DEPTH + 1),)),
        ],
        compiler_params=pltpu.CompilerParams(vmem_limit_bytes=12 * MIB),
        name="select",
    )(lists, *(near(p) for p in pieces))


def groups():
    out = []
    for s in range(0, SLOTS, 2):
        n = min(2, SLOTS - s)
        low = max(0, s - MID)
        high = min(SLOTS - 1, s + n - 1 + MID)
        out.append((s, n, low, high - low + 1))
    return out


GROUPS = groups()


def purify_kernel(lists, got, own, *refs):
    outs, (w, sq, out) = refs[:Y], refs[Y:]
    x, zl, zp, core, y = (lax.axis_index(a) for a in AXES)
    row = ROWS_HERE * ((x * Z + 2 * zl + zp) * CORE + core) + y

    def blk(a):
        return slice(a * BLK, (a + 1) * BLK)

    def sent(cls, place):
        tiles = [got[((t // Y) * ZP + cls) * Y + t % Y, place] for t in range(TILES)]
        return jnp.concatenate(tiles, axis=0)

    for a in range(SLOTS - HALF):
        w[blk(a), blk(a + HALF)] = jnp.zeros((BLK, BLK), jnp.bfloat16)
        w[blk(a + HALF), blk(a)] = jnp.zeros((BLK, BLK), jnp.bfloat16)
    for s in range(SLOTS):
        value = own[y, s]
        w[blk(MID), blk(s)] = value
        if s != MID:
            w[blk(s), blk(MID)] = value.T
    for cls in range(ZP):
        for place, (a, s) in enumerate(WANTED[cls]):
            value = sent(cls, place)
            w[blk(a), blk(s)] = value
            w[blk(s), blk(a)] = value.T
    for p in range(len(DIAGONAL) // 2):
        left, right = (sent(cls, BASE + p) for cls in range(ZP))
        a, s = DIAGONAL[2 * p], DIAGONAL[2 * p + 1]
        w[blk(a), blk(a)] = joined(left, turned(right))
        w[blk(s), blk(s)] = joined(turned(left), right)

    def mask(value, s):
        return jnp.where(lists[s, row] >= 0, value, jnp.zeros_like(value))

    def span(first, n):
        return slice(first * BLK, (first + n) * BLK)

    for s, n, low, count in GROUPS:
        total = jnp.dot(
            w[blk(MID), span(low, count)], w[span(low, count), span(s, n)], preferred_element_type=jnp.float32
        )
        for j in range(n):
            sq[:, blk(s + j)] = mask(total[:, blk(j)], s + j).astype(jnp.bfloat16)
    for s, n, low, count in GROUPS:
        total = jnp.dot(sq[:, span(low, count)], w[span(low, count), span(s, n)], preferred_element_type=jnp.float32)
        for j in range(n):
            value = 3.0 * sq[:, blk(s + j)].astype(jnp.float32) - 2.0 * total[:, blk(j)]
            value = mask(value, s + j).T.astype(jnp.bfloat16)
            for part in range(Y):
                out[part, s + j] = value[part * (BLK // Y) : (part + 1) * (BLK // Y)]
    for n in range(Y):
        outs[n][...] = out[(y + n) & (Y - 1)]


def purify(lists, got, own):
    return pl.pallas_call(
        purify_kernel,
        out_shape=[pltpu.VMEM((SLOTS, BLK // Y, BLK), jnp.bfloat16)] * Y,
        in_specs=[SMEM, VMEM, VMEM],
        out_specs=[VMEM] * Y,
        scratch_shapes=[
            pltpu.VMEM((SLOTS * BLK, SLOTS * BLK), jnp.bfloat16),
            pltpu.VMEM((BLK, SLOTS * BLK), jnp.bfloat16),
            pltpu.VMEM((Y, SLOTS, BLK // Y, BLK), jnp.bfloat16),
        ],
        compiler_params=pltpu.CompilerParams(vmem_limit_bytes=24 * MIB),
        name="purify",
    )(lists, near(got), near(own))


def place_kernel(own, one, two, three, out, sems):
    y = lax.axis_index("y")
    parts = (own, one, two, three)
    copies = [pltpu.make_async_copy(part, out.at[(y - n) & (Y - 1)], sems.at[n]) for n, part in enumerate(parts)]
    for copy in copies:
        copy.start()
    for copy in copies:
        copy.wait()


def place(strips, parts):
    return pl.pallas_call(
        place_kernel,
        out_shape=pltpu.HBM((Y, SLOTS, BLK // Y, BLK), jnp.bfloat16),
        in_specs=[VMEM] * Y,
        out_specs=pl.BlockSpec(memory_space=pltpu.HBM),
        scratch_shapes=[pltpu.SemaphoreType.DMA((Y,))],
        compiler_params=pltpu.CompilerParams(vmem_limit_bytes=4 * MIB),
        name="place",
    )(*(near(p) for p in (strips, *parts)))


def shifted(value, step):
    return lax.ppermute(value, "zl", [((i + step) % ZL, i) for i in range(ZL)])


def body(column_lists, block_values):
    lists = column_lists.T
    mine = pack(block_values).reshape(X * ZP, MESSAGE, TILE, BLK)
    part = lax.all_to_all(mine, ("x", "zp"), 0, 0, tiled=True).reshape(X, ZP, MESSAGE, TILE, BLK)
    ahead, behind = shifted(part, 1), shifted(part, -1)
    far = shifted(ahead[: X // 2], 1), shifted(behind[X // 2 :], -1)
    here = [part, ahead, behind, *far]
    near_pieces = lax.optimization_barrier((ahead, behind))
    there = [lax.ppermute(p, "core", [(0, 1), (1, 0)]) for p in (part, *near_pieces, *far)]
    asked = select(lists, here + there)
    got = lax.all_to_all(asked, ("x", "zp", "y"), 0, 0, tiled=True)
    strips = purify(lists, got, block_values)
    two, one, three = (
        lax.ppermute(strips[n], "y", [(i, (i + n) % Y) for i in range(Y)]) for n in (2, 1, 3)
    )
    mixed = place(strips[0], (one, two, three))
    return mixed.transpose(0, 1, 3, 2)


def solution(mesh):
    fine = Mesh(mesh.devices.reshape(X, ZL, ZP, CORE, Y), AXES)
    rows = ("x", "zl", "zp", "core")
    return jax.shard_map(
        body, mesh=fine, in_specs=(P(), P(rows)), out_specs=P(rows, None, None, "y"), check_vma=False
    )
```
